128 devices in a mesh: fsdp: 4 (over z_hi, core), ctx: 32 (over z_lo, x, y).
Axes of the slice: x: 4, y: 4, z: 4 (z_hi: 2, z_lo: 2; z = z_hi * 2 + z_lo), core: 2. Of those that a mesh axis runs over, the one named last changes fastest.
Arguments:
- tokens: bfloat16 [4, 16384, 8192], P('fsdp', 'ctx'), may hold values from -56 to 56
- codes: int32 [128, 20480], P('fsdp'), may hold values from 0 to 65535
- scales: bfloat16 [128, 1280], P('fsdp'), may hold values from 0.0039978027 to 0.039794922
- down_adapter_matrix: bfloat16 [128, 4096], P('fsdp'), may hold values from -0.0625 to 0.0625
- up_adapter_matrix: bfloat16 [64, 1280], replicated, may hold values from -0.75 to 0.75
- positions: int32 [4, 16384], P('fsdp', 'ctx'), may hold values from 0 to 16383, as said below
Outputs:
- attended: bfloat16 [4, 16384, 1024], P('fsdp', 'ctx')
The draws below stay inside these ranges and needn't reach their ends.
Inputs may be any that keep to these rules, and one draw needn't show every extreme that they name: In each sequence the first and the last 256 tokens of each device's share hold consecutive increasing positions, of some block a and of block 63 - a of the sequence (blocks of 256 positions), a different a on each device of a sequence; every position of 0 to 16383 appears once in each sequence.
All inputs are finite; a program needn't handle non-finite values.
Results may differ from the reference program's by a relative error of at most 0.014.
Values may be sent and summed in bfloat16 or wider, within the bound.
A program may use at most 192 MiB of HBM per device.

```python
import math
import jax
import jax.numpy as jnp
from jax import lax

MODEL_WIDTH = 8192
QH = 8
HD = 128
ADAPTER_RANK = 64
TOK_DEV = 512
SEQS = 4
SEQ = 16384
QUERY_KEY_VALUE = 1280


def draw_tokens(key, part):
    output_shape = (SEQS, SEQ, MODEL_WIDTH)
    return jnp.clip(jax.random.normal(key, output_shape, jnp.float32), -6.0, 6.0).astype(jnp.bfloat16)


def draw_positions(key, part):
    blocks = SEQ // TOK_DEV
    half_size = TOK_DEV // 2

    def one_sequence(sequence_index):
        order = jax.random.permutation(jax.random.fold_in(key, sequence_index), blocks).astype(jnp.int32)
        mirror = 2 * blocks - 1 - order
        offsets = jnp.arange(half_size, dtype=jnp.int32)
        first_part = order[:, None] * half_size + offsets[None, :]
        second_part = mirror[:, None] * half_size + offsets[None, :]
        return jnp.concatenate([first_part, second_part], axis=1).reshape(-1).astype(jnp.int32)
    return jax.vmap(one_sequence)(jnp.arange(SEQS, dtype=jnp.int32))


def place_ends(array, rng, low, high):
    extent = array.shape
    index_at = [jax.random.randint(jax.random.fold_in(rng, axis), (), 0, extent[axis]) for axis in range(len(extent))]
    array = array.at[tuple(index_at)].set(low)
    longest = extent.index(max(extent))
    index_at[longest] = (index_at[longest] + 1) % extent[longest]
    return array.at[tuple(index_at)].set(high)


def shard_levels(stream_key, extent, pieces, smallest, top_value):
    level, own = 1.0, jax.random.fold_in(stream_key, 6)
    for dim, blocks in pieces:
        steps = jnp.exp(jax.random.uniform(jax.random.fold_in(own, dim), (blocks,), jnp.float32, smallest / len(pieces), top_value / len(pieces)))
        level = level * jnp.repeat(steps, extent[dim] // blocks).reshape([-1 if axis == dim else 1 for axis in range(len(extent))])
    return level


def normal_values(key, dims, scale, bound, cuts=(), kind=jnp.bfloat16):
    level = shard_levels(key, dims, cuts, -0.22, 0.18) if cuts else 1.0
    drawn = jax.random.normal(key, dims, jnp.float32) * scale * level
    return jnp.minimum(jnp.maximum(drawn, -bound), bound).astype(kind)


def setup_inputs(seed: int = 0) -> dict:
    key_of = jax.random.split(jax.random.key(seed), 7)
    return {
        "tokens": draw_tokens(jax.random.fold_in(key_of[6], 71), 0),
        "codes": place_ends(jax.random.randint(key_of[1], (MODEL_WIDTH // 64, 16 * QUERY_KEY_VALUE), 0, 65536), jax.random.fold_in(key_of[1], 1), 0, 65535).astype(jnp.int32),
        "scales": jnp.clip(jnp.exp(math.log(0.039794922) - 2.2979944 * jax.random.uniform(key_of[2], (MODEL_WIDTH // 64, QUERY_KEY_VALUE), jnp.float32) ** shard_levels(key_of[2], (MODEL_WIDTH // 64, QUERY_KEY_VALUE), ((0, 4),), -0.2, 0.2)), 0.0039978027, 0.039794922).astype(jnp.bfloat16),
        "down_adapter_matrix": normal_values(key_of[3], (MODEL_WIDTH // 64, 64 * ADAPTER_RANK), MODEL_WIDTH ** -0.5, 0.0625, ((0, 4),)),
        "up_adapter_matrix": normal_values(key_of[4], (ADAPTER_RANK, QUERY_KEY_VALUE), ADAPTER_RANK ** -0.5, 0.75),
        "positions": draw_positions(jax.random.fold_in(key_of[6], 71), 0),
    }


normal_float_levels = [-1.0, -0.6961928009986877, -0.5250730514526367, -0.39491748809814453, -0.28444138169288635, -0.18477343022823334, -0.09105003625154495, 0.0, 0.07958029955625534, 0.16093020141124725, 0.24611230194568634, 0.33791524171829224, 0.44070982933044434, 0.5626170039176941, 0.7229568362236023, 1.0]
rope_base = 500000.0
adapter_scaling = 0.5


def unpack_codes(packed):
    blocks = packed.shape[0]
    words = packed.reshape(blocks, 64, -1)
    nibbles = [jnp.remainder(jnp.floor_divide(words, 16 ** place), 16) for place in range(4)]
    return jnp.stack(nibbles, axis=-1).reshape(blocks, 64, -1)


def pick_level(code_full):
    bit_flags = [jnp.remainder(jnp.floor_divide(code_full, 2 ** place), 2) == 1 for place in range(4)]
    current = [jnp.float32(level) for level in normal_float_levels]
    for place in range(4):
        current = [jnp.where(bit_flags[place], current[2 * pair + 1], current[2 * pair]) for pair in range(len(current) // 2)]
    return current[0]


def dequantize(packed, block_scales):
    code_full = unpack_codes(packed)
    values = pick_level(code_full)
    scaled = values * block_scales.astype(jnp.float32)[:, None, :]
    return scaled.reshape(-1, scaled.shape[-1]).astype(jnp.bfloat16)


def rotate_pairs(values, angles):
    half_size = values.shape[-1] // 2
    first_half = values[..., :half_size]
    second_half = values[..., half_size:]
    cosine = jnp.cos(angles)
    sine = jnp.sin(angles)
    return jnp.concatenate([first_half * cosine - second_half * sine, second_half * cosine + first_half * sine], axis=-1)


def make_angles(token_position):
    half_size = HD // 2
    steps_idx = jnp.arange(half_size, dtype=jnp.float32)
    inverse = jnp.exp(-jnp.log(jnp.float32(rope_base)) * 2.0 * steps_idx / HD)
    return token_position.astype(jnp.float32)[:, None] * inverse[None, :]


def project_inputs(sequence_tokens, weight_matrix, down_adapter_output, up_adapter_matrix, token_position):
    count = sequence_tokens.shape[0]
    base_output = jnp.dot(sequence_tokens, weight_matrix, preferred_element_type=jnp.float32)
    low_rank_output = jnp.dot(sequence_tokens, down_adapter_output, preferred_element_type=jnp.float32).astype(jnp.bfloat16)
    joined_output = base_output + adapter_scaling * jnp.dot(low_rank_output, up_adapter_matrix, preferred_element_type=jnp.float32)
    angles = make_angles(token_position)
    qwidth = QH * HD
    query_output = joined_output[:, :qwidth].reshape(count, QH, HD).transpose(1, 0, 2)
    query_output = (rotate_pairs(query_output, angles) * (HD ** -0.5)).astype(jnp.bfloat16)
    key = rotate_pairs(joined_output[:, qwidth:qwidth + HD], angles).astype(jnp.bfloat16)
    value_output = joined_output[:, qwidth + HD:].astype(jnp.bfloat16)
    return query_output, key, value_output


def attend(query_output, key, value_output, token_position):
    count = query_output.shape[1]
    qblock = math.gcd(count, 256)
    nblocks = count // qblock
    query_blocks = query_output.reshape(QH, nblocks, qblock, HD).transpose(1, 0, 2, 3)
    pos_blocks = token_position.reshape(nblocks, qblock)

    def one_block(packed_args):
        query_part, pos_part = packed_args
        scores = jnp.einsum('hqd,kd->hqk', query_part.astype(jnp.float32), key.astype(jnp.float32))
        scores = jnp.where(token_position[None, None, :] <= pos_part[None, :, None], scores, -jnp.inf)
        top = jnp.max(scores, axis=-1, keepdims=True)
        expo = jnp.exp(scores - top)
        total = jnp.sum(expo, axis=-1)
        weights = expo.astype(jnp.bfloat16)
        summed = jnp.einsum('hqk,kd->hqd', weights.astype(jnp.float32), value_output.astype(jnp.float32))
        return (summed / total[..., None]).astype(jnp.bfloat16)

    results = lax.map(one_block, (query_blocks, pos_blocks))
    return results.transpose(0, 2, 1, 3).reshape(count, QH * HD)


def reference(tokens, codes, scales, down_adapter_matrix, up_adapter_matrix, positions):
    weight_matrix = dequantize(codes, scales)
    down_adapter_output = down_adapter_matrix.reshape(-1, down_adapter_matrix.shape[1] // 64)
    results = []
    for sequence_index in range(tokens.shape[0]):
        query_output, key, value_output = project_inputs(tokens[sequence_index], weight_matrix, down_adapter_output, up_adapter_matrix, positions[sequence_index])
        results.append(attend(query_output, key, value_output, positions[sequence_index]))
    return jnp.stack(results)
```

```python
import jax
import jax.numpy as jnp
from jax import lax
from jax.experimental import pallas as pl
from jax.experimental.pallas import tpu as pltpu
from jax.sharding import PartitionSpec as P

MESH = pl.DeviceIdType.MESH
QH = 8
HD = 128
HEADS = QH + 2
HALF = 256
TOK = 512
WIDTH = 8192
OUT = 1280
ROWS = 2048
RANK = 64
META = 16
PIECE = 512 + META
ROPE_BASE = 500000.0
LEVELS = (
    -1.0, -0.6961928009986877, -0.5250730514526367, -0.39491748809814453,
    -0.28444138169288635, -0.18477343022823334, -0.09105003625154495, 0.0,
    0.07958029955625534, 0.16093020141124725, 0.24611230194568634, 0.33791524171829224,
    0.44070982933044434, 0.5626170039176941, 0.7229568362236023, 1.0,
)
F32 = jnp.float32
BF16 = jnp.bfloat16
NT = (((1,), (1,)), ((), ()))
NEG = -1e30


def iota(shape, dim):
    return lax.broadcasted_iota(jnp.int32, shape, dim)


def head_order():
    p = iota((HD, HD), 1)
    return jnp.where(iota((HD, HD), 0) == 4 * (p % 32) + p // 32, 1.0, 0.0).astype(BF16)


def dequant_kernel(codes, scales, up, w_out, up_out, raw, nat, sc, sems):
    b = pl.program_id(0)

    def fetch(i):
        return pltpu.make_async_copy(codes.at[i // 8, :, i % 8, :], raw.at[i], sems.at[i])

    @pl.when(b == 0)
    def _():
        def start(i, carry):
            fetch(i).start()
            return carry

        lax.fori_loop(0, 32, start, 0)
        order = head_order()
        for h in range(HEADS):
            cols = slice(h * HD, (h + 1) * HD)
            sc[h] = jnp.dot(scales[:, cols], order, preferred_element_type=F32)
            up_out[:, cols] = jnp.dot(up[:, cols], order, preferred_element_type=F32).astype(BF16)

    fetch(b).wait()
    left = iota((8, 128), 1) < 64
    for g in range(4):
        u = [raw[b, pl.ds(40 * g + i, 8, stride=5), :] for i in range(5)]
        r2, r3, r4 = (pltpu.roll(u[i], 64, 1) for i in (2, 3, 4))
        for j in range(3):
            nat[j, pl.ds(16 * g, 8, stride=2), :] = u[j]
        odd = (jnp.where(left, r2, r3), jnp.where(left, r3, r4), r4)
        for j in range(3):
            nat[j, pl.ds(16 * g + 1, 8, stride=2), :] = odd[j]
    lane = iota((64, 128), 1)
    shift = 4 * (lane // 32)
    small = iota((64, 128), 1) % 16
    table = jnp.zeros((64, 128), F32)
    for n, level in enumerate(LEVELS):
        table = jnp.where(small == n, level, table)
    for h in range(HEADS):
        j, t = h // 4, h % 4
        words = nat[j]
        words = jnp.take_along_axis(words, lane % 32 + 32 * t, axis=1, mode="promise_in_bounds")
        code = (words >> shift) & 15
        level = jnp.take_along_axis(table, code, axis=1, mode="promise_in_bounds")
        cols = slice(h * HD, (h + 1) * HD)
        w_out[:, cols] = (level * sc[h, pl.ds(b, 1), :]).astype(BF16)


def dequant(codes, scales, up):
    view = codes.reshape(4, 8, 160, 128).transpose(0, 2, 1, 3)
    whole = lambda shape: pl.BlockSpec(shape, lambda b: (0, 0))
    return pl.pallas_call(
        dequant_kernel,
        grid=(32,),
        out_shape=(
            jax.ShapeDtypeStruct((ROWS, OUT), BF16),
            jax.ShapeDtypeStruct((RANK, OUT), BF16),
        ),
        in_specs=[pl.BlockSpec(memory_space=pl.ANY), whole((32, OUT)), whole((RANK, OUT))],
        out_specs=(pl.BlockSpec((64, OUT), lambda b: (b, 0)), whole((RANK, OUT))),
        scratch_shapes=[
            pltpu.VMEM((32, 160, 128), jnp.int32),
            pltpu.VMEM((3, 64, 128), jnp.int32),
            pltpu.VMEM((HEADS, 32, HD), F32),
            pltpu.SemaphoreType.DMA((32,)),
        ],
        compiler_params=pltpu.CompilerParams(vmem_limit_bytes=32 << 20),
        name="dequant",
    )(view, scales, up)


def place():
    f, c = lax.axis_index("fsdp"), lax.axis_index("ctx")
    return f // 2, f % 2, c // 16, (c // 4) % 4, c % 4


def device(z_hi, core, z_lo, x, y):
    return (z_hi * 2 + core, z_lo * 16 + (x % 4) * 4 + y % 4)


def project_kernel(
    pos, tok_hbm, w_hbm, d_hbm, up, q_out, kv_out,
    wbuf, dbuf, tok, acc, accd, cos_ref, sin_ref,
    local, wsend, wrecv, dsend, drecv,
):
    z_hi, core, z_lo, x, y = place()
    z = z_hi * 2 + z_lo
    cross_z = jnp.where(z % 2 == 0, (z + 3) % 4, (z + 1) % 4)
    cross = device(cross_z // 2, core, cross_z % 2, x, y)
    partner = device(z_hi, 1 - core, z_lo, x, y)
    xp, xm = device(z_hi, core, z_lo, x + 1, y), device(z_hi, core, z_lo, x + 3, y)
    yp, ym = device(z_hi, core, z_lo, x, y + 1), device(z_hi, core, z_lo, x, y + 3)
    col = (x + 2 * y) % 4

    tok_copy = pltpu.make_async_copy(tok_hbm, tok, local.at[0])
    own_w = pltpu.make_async_copy(w_hbm, wbuf.at[0], local.at[1])
    own_d = pltpu.make_async_copy(d_hbm, dbuf.at[0], local.at[2])
    own_w.start()
    own_d.start()
    tok_copy.start()

    barrier = pltpu.get_barrier_semaphore()
    for peer in (cross, partner, xp, xm, yp, ym):
        pl.semaphore_signal(barrier, inc=1, device_id=peer, device_id_type=MESH)
    pl.semaphore_wait(barrier, 6)

    shift = (0, 3, 1, 2)

    def rows_of(k, c):
        quarter = (col + shift[k]) % 4
        return pl.ds(pl.multiple_of(quarter * 512 + c * 128, 128), 128)

    def drows_of(k):
        quarter = (col + shift[k]) % 4
        return pl.ds(pl.multiple_of(quarter * 256, 256), 256)

    def wcopy(kind, c, src, dst, peer):
        return pltpu.make_async_remote_copy(
            src_ref=src, dst_ref=dst, send_sem=wsend.at[kind, c], recv_sem=wrecv.at[kind, c],
            device_id=peer, device_id_type=MESH,
        )

    def dcopy(kind, src, dst, peer):
        return pltpu.make_async_remote_copy(
            src_ref=src, dst_ref=dst, send_sem=dsend.at[kind], recv_sem=drecv.at[kind],
            device_id=peer, device_id_type=MESH,
        )

    def w_of(kind, c):
        if kind == 0:
            rows = rows_of(0, c)
            return wcopy(0, c, w_hbm.at[rows, :], wbuf.at[2, rows, :], cross)
        if kind in (1, 2, 3):
            rows = rows_of(0, c)
            peer = xp if kind == 1 else xm if kind == 2 else (yp, ym)[c % 2]
            return wcopy(kind, c, wbuf.at[2, rows, :], wbuf.at[2, rows, :], peer)
        if kind == 4:
            rows = pl.ds(c * 512, 512)
            return wcopy(4, c, w_hbm.at[rows, :], wbuf.at[1, rows, :], partner)
        rows = rows_of(kind - 5, c)
        return wcopy(kind, c, wbuf.at[2, rows, :], wbuf.at[3, rows, :], partner)

    def d_of(kind):
        if kind == 0:
            rows = drows_of(0)
            return dcopy(0, d_hbm.at[rows, :], dbuf.at[2, rows, :], cross)
        if kind in (1, 2, 3):
            rows = drows_of(0)
            return dcopy(kind, dbuf.at[2, rows, :], dbuf.at[2, rows, :], (xp, xm, yp)[kind - 1])
        if kind == 4:
            return dcopy(4, d_hbm, dbuf.at[1], partner)
        rows = drows_of(kind - 5)
        return dcopy(kind, dbuf.at[2, rows, :], dbuf.at[3, rows, :], partner)

    for c in range(4):
        w_of(0, c).start()
        if c == 0:
            d_of(0).start()
        w_of(4, c).start()
    d_of(4).start()

    half = HD // 2
    lane = iota((TOK, HD), 1)
    row = iota((TOK, HD), 0)
    index = (4 * (lane % 16) + lane // 32).astype(F32)
    inverse = jnp.exp(-jnp.log(F32(ROPE_BASE)) * 2.0 * index / HD)
    token_pos = jnp.where(row < HALF, row + pos[0, 0], row - HALF + pos[0, HALF])
    angle = token_pos.astype(F32) * inverse
    cos_ref[...] = jnp.cos(angle)
    sin_ref[...] = jnp.where(lane % 32 < 16, -1.0, 1.0) * jnp.sin(angle)

    acc[...] = jnp.zeros_like(acc)
    accd[...] = jnp.zeros_like(accd)
    tok_copy.wait()
    own_w.wait()
    own_d.wait()

    def arrive(c):
        w_of(0, c).wait_recv()
        for kind in (1, 2, 3, 5):
            w_of(kind, c).start()
        if c == 0:
            d_of(0).wait_recv()
            for kind in (1, 2, 3, 5):
                d_of(kind).start()

    def onward(c):
        for kind in (1, 2, 3):
            w_of(kind, c).wait_recv()
            w_of(5 + kind, c).start()
        if c == 0:
            for kind in (1, 2, 3):
                d_of(kind).wait_recv()
                d_of(5 + kind).start()

    def from_partner(kinds, cs):
        for kind in kinds:
            for c in cs:
                w_of(5 + kind, c).wait_recv()
            if 0 in cs:
                d_of(5 + kind).wait_recv()

    def events(u):
        def at(k):
            return pl.when(u == k)

        for k in range(4):
            @at(8 + 2 * k)
            def _():
                w_of(4, k).wait_recv()
                if k == 0:
                    d_of(4).wait_recv()

        @at(11)
        def _():
            arrive(0)

        @at(16)
        def _():
            arrive(1)

        @at(17)
        def _():
            onward(0)
            arrive(2)
            onward(1)

        @at(20)
        def _():
            from_partner((0,), (0, 1))

        @at(21)
        def _():
            from_partner((1, 2, 3), (0, 1))
            onward(2)
            arrive(3)

        @at(25)
        def _():
            onward(3)

        @at(28)
        def _():
            from_partner((0, 1, 2, 3), (2, 3))

    def unit(u, carry):
        events(u)
        late = u >= 16
        v = u % 8
        slot = jnp.where(late, 2 + (v // 4), u // 8)
        kind = v % 4
        moved = jnp.where(kind == 1, 3, jnp.where(kind == 2, 1, jnp.where(kind == 3, 2, 0)))
        quarter = jnp.where(late, (col + moved) % 4, v // 2)
        part = jnp.where(late, (u - 16) // 8, v % 2)
        base = quarter * 512 + part * 256
        other = 1 - z_hi
        owner = jnp.where(slot == 0, z_hi * 2 + core, jnp.where(
            slot == 1, z_hi * 2 + 1 - core, jnp.where(slot == 2, other * 2 + core, other * 2 + 1 - core)))
        t = tok[:, pl.ds(pl.multiple_of(owner * ROWS + base, 256), 256)]
        acc[...] += jnp.dot(
            t, wbuf[slot, pl.ds(pl.multiple_of(base, 256), 256), :], preferred_element_type=F32)
        accd[part] += jnp.dot(
            t, dbuf[slot, pl.ds(pl.multiple_of(quarter * 256, 256), 256), :], preferred_element_type=F32)
        return carry

    lax.fori_loop(0, 32, unit, 0)

    low = (accd[0] + pltpu.roll(accd[1], half, 1)).astype(BF16)[:, :RANK]
    start0, start1 = pos[0, 0], pos[0, HALF]
    swap = start0 > start1
    lower = jnp.where(swap, start1, start0)
    first = lane % 32 < 16
    eye = jnp.where(iota((HD, HD), 0) == iota((HD, HD), 1), 1.0, 0.0).astype(BF16)
    order = head_order()

    def joined(h):
        cols = slice(h * HD, (h + 1) * HD)
        return acc[:, cols] + 0.5 * jnp.dot(low, up[:, cols], preferred_element_type=F32)

    def rope(u):
        pair = jnp.where(first, pltpu.roll(u, HD - 16, 1), pltpu.roll(u, 16, 1))
        return u * cos_ref[...] + pair * sin_ref[...]

    def halves(a, axis):
        lo = lax.slice_in_dim(a, 0, HALF, axis=axis)
        hi = lax.slice_in_dim(a, HALF, TOK, axis=axis)
        return jnp.where(swap, hi, lo), jnp.where(swap, lo, hi)

    for h in range(QH):
        q = (rope(joined(h)) * HD ** (-0.5)).astype(BF16)
        qt = lax.dot_general(eye, q, NT, preferred_element_type=F32)
        for s, part in enumerate(halves(qt, 1)):
            q_out[s, :, h * HALF : (h + 1) * HALF] = part.astype(BF16)
    for s, part in enumerate(halves(rope(joined(QH)), 0)):
        kv_out[s, :HALF, :] = part.astype(BF16)
    v = joined(QH + 1).astype(BF16)
    vt = lax.dot_general(order, v, NT, preferred_element_type=F32)
    for s, part in enumerate(halves(vt, 1)):
        kv_out[s, HALF : HALF + 128, :] = part[:, :128].astype(BF16)
        kv_out[s, HALF + 128 : HALF + 256, :] = part[:, 128:].astype(BF16)
        kv_out[s, 2 * HALF :, :] = (jnp.zeros((META, HD), F32) + (lower // HALF).astype(F32)).astype(BF16)

    for c in range(4):
        for kind in range(9):
            w_of(kind, c).wait_send()
    for kind in range(9):
        d_of(kind).wait_send()


def project(pos, tokens, weight, down, up):
    anywhere = pl.BlockSpec(memory_space=pl.ANY)
    vmem = pl.BlockSpec(memory_space=pltpu.VMEM)
    dma = pltpu.SemaphoreType.DMA
    return pl.pallas_call(
        project_kernel,
        out_shape=(
            jax.ShapeDtypeStruct((2, HD, QH * HALF), BF16),
            jax.ShapeDtypeStruct((2, PIECE, HD), BF16),
        ),
        in_specs=[pl.BlockSpec(memory_space=pltpu.SMEM), anywhere, anywhere, anywhere, vmem],
        out_specs=(vmem, vmem),
        scratch_shapes=[
            pltpu.VMEM((4, ROWS, OUT), BF16),
            pltpu.VMEM((4, ROWS // 2, HD), BF16),
            pltpu.VMEM((TOK, WIDTH), BF16),
            pltpu.VMEM((TOK, OUT), F32),
            pltpu.VMEM((2, TOK, HD), F32),
            pltpu.VMEM((TOK, HD), F32),
            pltpu.VMEM((TOK, HD), F32),
            dma((3,)), dma((9, 4)), dma((9, 4)), dma((9,)), dma((9,)),
        ],
        compiler_params=pltpu.CompilerParams(
            collective_id=0, has_side_effects=True, vmem_limit_bytes=60 << 20),
        name="project",
    )(pos, tokens, weight, down, up)


ORDER = (
    (0, 0, 0), (0, 1, 0), (0, 3, 0), (0, 0, 1), (0, 0, 3), (1, 0, 0), (0, 2, 0), (0, 0, 2),
    (0, 1, 3), (0, 1, 1), (0, 3, 3), (1, 1, 0), (0, 3, 1), (1, 3, 0), (0, 2, 1), (1, 0, 1),
    (0, 2, 3), (0, 1, 2), (1, 0, 3), (1, 3, 1), (1, 1, 1), (0, 3, 2), (1, 3, 3), (1, 1, 3),
    (1, 2, 0), (1, 2, 1), (0, 2, 2), (1, 0, 2), (1, 2, 3), (1, 3, 2), (1, 1, 2), (1, 2, 2),
)
SLOT = {s: i for i, s in enumerate(ORDER)}
BLOCKS = len(ORDER)
AHEAD = 1


def routes():
    table = {}
    for p in (0, 1):
        table[(0, 1, 0), p] = ("xp", (0, 0, 0))
        table[(0, 3, 0), p] = ("xm", (0, 0, 0))
        for dx in range(4):
            table[(0, dx, 1), p] = ("yp", (0, dx, 0))
            table[(0, dx, 3), p] = ("ym", (0, dx, 0))
        for s in ((0, 0), (1, 0), (3, 0), (2, 0), (0, 1), (0, 3)):
            table[(1,) + s, p] = ("z", (0,) + s)
        for dy in (1, 2, 3):
            table[(1, 1, dy), p] = ("xp", (1, 0, dy))
            table[(1, 3, dy), p] = ("xm", (1, 0, dy))
    table[(0, 2, 0), 0] = ("xm", (0, 3, 0))
    table[(0, 2, 0), 1] = ("xp", (0, 1, 0))
    for dx in range(4):
        table[(0, dx, 2), 0] = ("ym", (0, dx, 3))
        table[(0, dx, 2), 1] = ("yp", (0, dx, 1))
    table[(1, 0, 2), 0] = ("ym", (1, 0, 3))
    table[(1, 0, 2), 1] = ("yp", (1, 0, 1))
    for dy in (1, 2, 3):
        table[(1, 2, dy), 0] = ("xm", (1, 3, dy))
        table[(1, 2, dy), 1] = ("xp", (1, 1, dy))
    return table


def forwards():
    opposite = {"xp": "xm", "xm": "xp", "yp": "ym", "ym": "yp", "z": "z"}
    table = {i: [] for i in range(BLOCKS)}
    for (s, p), (origin, source) in routes().items():
        table[SLOT[source]].append((SLOT[s], p, opposite[origin]))
    return {i: sorted(v) for i, v in table.items()}


def attend_kernel(pos, q, kv, out, kvbuf, k2, vt1, vt2, m_ref, acc, local, send, recv):
    z_hi, core, z_lo, x, y = place()
    peers = {
        "xp": device(z_hi, core, z_lo, x + 1, y), "xm": device(z_hi, core, z_lo, x + 3, y),
        "yp": device(z_hi, core, z_lo, x, y + 1), "ym": device(z_hi, core, z_lo, x, y + 3),
        "z": device(z_hi, core, 1 - z_lo, x, y),
    }
    table = forwards()
    own = pltpu.make_async_copy(kv, kvbuf.at[0], local.at[0])
    own.start()
    barrier = pltpu.get_barrier_semaphore()
    for peer in peers.values():
        pl.semaphore_signal(barrier, inc=1, device_id=peer, device_id_type=MESH)
    pl.semaphore_wait(barrier, len(peers))
    own.wait()

    def copy(source, slot, piece, peer):
        return pltpu.make_async_remote_copy(
            src_ref=kvbuf.at[source, piece], dst_ref=kvbuf.at[slot, piece],
            send_sem=send.at[slot, piece], recv_sem=recv.at[slot, piece],
            device_id=peer, device_id_type=MESH,
        )

    def forward(source):
        for slot, piece, to in table[source]:
            copy(source, slot, piece, peers[to]).start()

    def take(slot):
        for piece in range(2):
            copy(0, slot, piece, peers["z"]).wait_recv()

    forward(0)

    start0, start1 = pos[0, 0], pos[0, HALF]
    swap = start0 > start1
    mine = (jnp.where(swap, start1, start0) // HALF).astype(F32)
    vt1[HD:, :] = jnp.ones((META, HALF), BF16)
    vt2[HD:, :] = jnp.ones((META, HALF), BF16)

    def keys(slot, piece):
        return kvbuf[slot, piece, :HALF, :]

    def values(slot, piece):
        return jnp.concatenate(
            [kvbuf[slot, piece, HALF : HALF + 128, :], kvbuf[slot, piece, HALF + 128 : HALF + 256, :]], axis=1)

    def scores(k, qt):
        return jnp.dot(k, qt, preferred_element_type=F32)

    def weigh(vt, s, m):
        return jnp.dot(vt, jnp.exp(s - m).astype(BF16), preferred_element_type=F32)

    def top(s):
        return jnp.max(s, axis=0, keepdims=True)

    vt1[:HD, :] = values(0, 0)
    vt2[:HD, :] = values(0, 1)
    k2[...] = keys(0, 1)

    def own_head(h, carry):
        cols = pl.ds(pl.multiple_of(h * HALF, HALF), HALF)
        q0, q1 = q[0, :, cols], q[1, :, cols]
        seen = iota((HALF, HALF), 0) <= iota((HALF, HALF), 1)
        s00 = jnp.where(seen, scores(keys(0, 0), q0), -jnp.inf)
        m0 = top(s00)
        m_ref[0, h] = jnp.broadcast_to(m0, (8, HALF))
        acc[0, h] = weigh(vt1[...], s00, m0)
        s10 = scores(keys(0, 0), q1)
        s11 = jnp.where(seen, scores(k2[...], q1), -jnp.inf)
        m1 = jnp.maximum(top(s10), top(s11))
        m_ref[1, h] = jnp.broadcast_to(m1, (8, HALF))
        acc[1, h] = weigh(vt1[...], s10, m1) + weigh(vt2[...], s11, m1)
        return carry

    lax.fori_loop(0, QH, own_head, 0)

    def step(i, carry):
        for k in range(1, BLOCKS):
            if table[k]:
                @pl.when(i + AHEAD == k)
                def _():
                    take(k)
                    forward(k)
            else:
                @pl.when(i + AHEAD == k)
                def _():
                    take(k)

        @pl.when(i > 0)
        def _():
            theirs = jnp.max(kvbuf[i, 0, 2 * HALF :, :].astype(F32))
            c = theirs < mine
            lo_bias = jnp.where(c, 0.0, NEG)
            hi_bias = jnp.where(c, NEG, 0.0)
            w_lo = jnp.where(c, 1.0, 0.0)
            w_hi = jnp.where(c, 0.0, 1.0)
            k2[...] = jnp.where(c, keys(i, 0), keys(i, 1))
            vt1[:HD, :] = values(i, 0)
            vt2[:HD, :] = jnp.where(c, values(i, 0), values(i, 1))

            def head(h, carry):
                cols = pl.ds(pl.multiple_of(h * HALF, HALF), HALF)
                q1 = q[1, :, cols]
                q2 = jnp.where(c, q[0, :, cols], q1)
                s1 = scores(keys(i, 0), q1)
                s2 = scores(k2[...], q2)
                t1, t2 = top(s1), top(s2)
                m_lo, m_hi = m_ref[0, h, :1, :], m_ref[1, h, :1, :]
                n_lo = jnp.maximum(m_lo, t2 + lo_bias)
                n_hi = jnp.maximum(m_hi, jnp.maximum(t1, t2 + hi_bias))
                o1 = weigh(vt1[...], s1, n_hi)
                o2 = weigh(vt2[...], s2, jnp.where(c, n_lo, n_hi))
                f_lo, f_hi = jnp.exp(m_lo - n_lo), jnp.exp(m_hi - n_hi)
                m_ref[0, h] = jnp.broadcast_to(n_lo, (8, HALF))
                m_ref[1, h] = jnp.broadcast_to(n_hi, (8, HALF))
                acc[0, h] = acc[0, h] * f_lo + o2 * w_lo
                acc[1, h] = acc[1, h] * f_hi + (o1 + o2 * w_hi)
                return carry

            lax.fori_loop(0, QH, head, 0)

        return carry

    lax.fori_loop(1 - AHEAD, BLOCKS, step, 0)

    for h in range(QH):
        cols = slice(h * HD, (h + 1) * HD)
        parts = []
        for s in range(2):
            total = acc[s, h, HD : HD + 1, :]
            parts.append((acc[s, h, :HD, :] / total).T)
        out[:HALF, cols] = jnp.where(swap, parts[1], parts[0]).astype(BF16)
        out[HALF:, cols] = jnp.where(swap, parts[0], parts[1]).astype(BF16)

    def drain(slot, carry):
        for piece in range(2):
            copy(0, slot, piece, peers["z"]).wait_send()
        return carry

    lax.fori_loop(1, BLOCKS, drain, 0)


def attend(pos, q, kv):
    anywhere = pl.BlockSpec(memory_space=pl.ANY)
    vmem = pl.BlockSpec(memory_space=pltpu.VMEM)
    dma = pltpu.SemaphoreType.DMA
    return pl.pallas_call(
        attend_kernel,
        out_shape=jax.ShapeDtypeStruct((TOK, QH * HD), BF16),
        in_specs=[pl.BlockSpec(memory_space=pltpu.SMEM), vmem, anywhere],
        out_specs=vmem,
        scratch_shapes=[
            pltpu.VMEM((BLOCKS, 2, PIECE, HD), BF16),
            pltpu.VMEM((HALF, HD), BF16),
            pltpu.VMEM((HD + META, HALF), BF16),
            pltpu.VMEM((HD + META, HALF), BF16),
            pltpu.VMEM((2, QH, 8, HALF), F32),
            pltpu.VMEM((2, QH, HD + META, HALF), F32),
            dma((1,)), dma((BLOCKS, 2)), dma((BLOCKS, 2)),
        ],
        compiler_params=pltpu.CompilerParams(
            collective_id=1, has_side_effects=True, vmem_limit_bytes=60 << 20),
        name="attend",
    )(pos, q, kv)


def on_device(tokens, codes, scales, down_adapter_matrix, up_adapter_matrix, positions):
    weight, up = dequant(codes, scales, up_adapter_matrix)
    down = down_adapter_matrix.reshape(4, 2, HALF, RANK).transpose(0, 2, 1, 3).reshape(ROWS // 2, HD)
    q, kv = project(positions, tokens[0], weight, down, up)
    return attend(positions, q, kv)[None]


def solution(mesh):
    return jax.shard_map(
        on_device,
        mesh=mesh,
        in_specs=(
            P("fsdp", "ctx", None), P("fsdp", None), P("fsdp", None), P("fsdp", None), P(), P("fsdp", "ctx"),
        ),
        out_specs=P("fsdp", "ctx", None),
        check_vma=False,
    )
```

```python
import jax
import jax.numpy as jnp
from jax import lax
from jax.experimental import pallas as pl
from jax.experimental.pallas import tpu as pltpu
from jax.sharding import PartitionSpec as P

MESH = pl.DeviceIdType.MESH
QH = 8
HD = 128
HEADS = QH + 2
HALF = 256
TOK = 512
WIDTH = 8192
OUT = 1280
ROWS = 2048
RANK = 64
META = 16
PIECE = 512 + META
ROPE_BASE = 500000.0
LEVELS = (
    -1.0, -0.6961928009986877, -0.5250730514526367, -0.39491748809814453,
    -0.28444138169288635, -0.18477343022823334, -0.09105003625154495, 0.0,
    0.07958029955625534, 0.16093020141124725, 0.24611230194568634, 0.33791524171829224,
    0.44070982933044434, 0.5626170039176941, 0.7229568362236023, 1.0,
)
F32 = jnp.float32
BF16 = jnp.bfloat16
NT = (((1,), (1,)), ((), ()))
NEG = -1e30
LOG2E = 1.4426950408889634


def iota(shape, dim):
    return lax.broadcasted_iota(jnp.int32, shape, dim)


def head_order():
    p = iota((HD, HD), 1)
    return jnp.where(iota((HD, HD), 0) == 4 * (p % 32) + p // 32, 1.0, 0.0).astype(BF16)


def plane(t):
    depth = 512 if t < 8 else 256
    lane = iota((depth, HD), 1)
    column = 4 * lane + t % 4 if t < 8 else 4 * (lane % 64) + 2 * (t - 8) + lane // 64
    return (t // 4) * 512, jnp.where(iota((depth, HD), 0) == column, 1.0, 0.0).astype(BF16)


def lookup(tables, words, move):
    numbers = lax.GatherDimensionNumbers(
        offset_dims=(), collapsed_slice_dims=(0,), start_index_map=(0,),
        operand_batching_dims=(1,), start_indices_batching_dims=(1,))
    index = (words >> move) & 7
    low, high = (
        lax.gather(t, index[..., None], numbers, slice_sizes=(1, 1), mode=lax.GatherScatterMode.PROMISE_IN_BOUNDS)
        for t in tables)
    return jnp.where((words & (8 << move)) != 0, high, low)


def place():
    f, c = lax.axis_index("fsdp"), lax.axis_index("ctx")
    return f // 2, f % 2, c // 16, (c // 4) % 4, c % 4


def device(z_hi, core, z_lo, x, y):
    return (z_hi * 2 + core, z_lo * 16 + (x % 4) * 4 + y % 4)


def project_kernel(
    pos, tok_hbm, codes, scales, d_hbm, up_in, q_out, kv_out,
    wbuf, dbuf, tok, acc, accd, cos_ref, sin_ref, raw, nat, sc, up,
    local, fetched, wsend, wrecv, dsend, drecv,
):
    z_hi, core, z_lo, x, y = place()
    z = z_hi * 2 + z_lo
    cross_z = jnp.where(z % 2 == 0, (z + 3) % 4, (z + 1) % 4)
    cross = device(cross_z // 2, core, cross_z % 2, x, y)
    partner = device(z_hi, 1 - core, z_lo, x, y)
    xp, xm = device(z_hi, core, z_lo, x + 1, y), device(z_hi, core, z_lo, x + 3, y)
    yp, ym = device(z_hi, core, z_lo, x, y + 1), device(z_hi, core, z_lo, x, y + 3)
    col = (x + 2 * y) % 4

    def block(n):
        return (col * 8 + n) % 32

    def fetch(n):
        b = block(n)
        return pltpu.make_async_copy(codes.at[b // 8, :, b % 8, :], raw.at[b], fetched.at[n])

    def start(n, carry):
        fetch(n).start()
        return carry

    lax.fori_loop(0, 32, start, 0)
    tok_copy = pltpu.make_async_copy(tok_hbm, tok, local.at[0])
    own_d = pltpu.make_async_copy(d_hbm, dbuf.at[0], local.at[1])
    own_d.start()
    tok_copy.start()

    barrier = pltpu.get_barrier_semaphore()
    for peer in (cross, partner, xp, xm, yp, ym):
        pl.semaphore_signal(barrier, inc=1, device_id=peer, device_id_type=MESH)

    for t in range(HEADS):
        first, picks = plane(t)
        cols = slice(first, first + picks.shape[0])
        sc[t] = jnp.dot(scales[:, cols], picks, preferred_element_type=F32)
        half_up = 0.5 * jnp.dot(up_in[:, cols], picks, preferred_element_type=F32)
        up[:, t * HD : (t + 1) * HD] = half_up.astype(BF16)
    pl.semaphore_wait(barrier, 6)

    shift = (0, 3, 1, 2)

    def rows_of(k, c):
        quarter = (col + shift[k]) % 4
        return pl.ds(pl.multiple_of(quarter * 512 + c * 128, 128), 128)

    def drows_of(k):
        quarter = (col + shift[k]) % 4
        return pl.ds(pl.multiple_of(quarter * 256, 256), 256)

    def wcopy(kind, c, src, dst, peer):
        return pltpu.make_async_remote_copy(
            src_ref=src, dst_ref=dst, send_sem=wsend.at[kind, c], recv_sem=wrecv.at[kind, c],
            device_id=peer, device_id_type=MESH,
        )

    def dcopy(kind, src, dst, peer):
        return pltpu.make_async_remote_copy(
            src_ref=src, dst_ref=dst, send_sem=dsend.at[kind], recv_sem=drecv.at[kind],
            device_id=peer, device_id_type=MESH,
        )

    def w_of(kind, c):
        if kind == 0:
            rows = rows_of(0, c)
            return wcopy(0, c, wbuf.at[0, rows, :], wbuf.at[2, rows, :], cross)
        if kind in (1, 2, 3):
            rows = rows_of(0, c)
            peer = xp if kind == 1 else xm if kind == 2 else (yp, ym)[c % 2]
            return wcopy(kind, c, wbuf.at[2, rows, :], wbuf.at[2, rows, :], peer)
        if kind == 4:
            rows = pl.ds(pl.multiple_of((col + c) % 4 * 512, 512), 512)
            return wcopy(4, c, wbuf.at[0, rows, :], wbuf.at[1, rows, :], partner)
        rows = rows_of(kind - 5, c)
        return wcopy(kind, c, wbuf.at[2, rows, :], wbuf.at[3, rows, :], partner)

    def d_of(kind):
        if kind == 0:
            rows = drows_of(0)
            return dcopy(0, d_hbm.at[rows, :], dbuf.at[2, rows, :], cross)
        if kind in (1, 2, 3):
            rows = drows_of(0)
            return dcopy(kind, dbuf.at[2, rows, :], dbuf.at[2, rows, :], (xp, xm, yp)[kind - 1])
        if kind == 4:
            return dcopy(4, d_hbm, dbuf.at[1], partner)
        rows = drows_of(kind - 5)
        return dcopy(kind, dbuf.at[2, rows, :], dbuf.at[3, rows, :], partner)

    d_of(0).start()
    d_of(4).start()

    left = iota((8, HD), 1) < 64
    place_in = iota((64, HD), 1)
    digit = 4 * (place_in // 64)
    tables = []
    for first in (0, 8):
        table = jnp.zeros((8, HD), F32)
        for n in range(8):
            table = jnp.where(iota((8, HD), 0) == n, LEVELS[first + n], table)
        tables.append(table)

    def dequantize(n, slot):
        b = block(n)
        fetch(n).wait()
        for g in range(4):
            u = [raw[b, pl.ds(40 * g + i, 8, stride=5), :] for i in range(5)]
            r2, r3, r4 = (pltpu.roll(u[i], 64, 1) for i in (2, 3, 4))
            odd = (jnp.where(left, r2, r3), jnp.where(left, r3, r4), r4)
            for j in range(3):
                nat[slot, j, pl.ds(16 * g, 8, stride=2), :] = u[j]
                nat[slot, j, pl.ds(16 * g + 1, 8, stride=2), :] = odd[j]

    def levels(n, slot):
        b = block(n)
        rows = pl.ds(pl.multiple_of(b * 64, 64), 64)
        for t in range(HEADS):
            words = nat[slot, t // 4]
            if t < 8:
                move = 4 * (t % 4)
            else:
                words = jnp.where(place_in < 64, words, pltpu.roll(words, 64, 1))
                move = digit + 8 * (t - 8)
            level = jnp.concatenate(
                [lookup(tables, words[r : r + 8], move if t < 8 else move[:8]) for r in range(0, 64, 8)], axis=0)
            wbuf[0, rows, t * HD : (t + 1) * HD] = (level * sc[t, pl.ds(b, 1), :]).astype(BF16)

    def pair(n, carry):
        dequantize(2 * n, 0)
        dequantize(2 * n + 1, 1)
        levels(2 * n, 0)
        levels(2 * n + 1, 1)

        @pl.when(n <= 4)
        def _():
            for c in range(4):
                @pl.when(n == c + 1)
                def _():
                    w_of(0, c).start()

        @pl.when((n > 0) & (n % 4 == 0))
        def _():
            for c in range(3):
                @pl.when(n == 4 * c + 4)
                def _():
                    w_of(4, c).start()

        return carry

    lax.fori_loop(0, 16, pair, 0)

    row = iota((64, TOK), 0)
    lane = iota((64, TOK), 1)
    index = (4 * (row % 16) + row // 16).astype(F32)
    inverse = jnp.exp(-jnp.log(F32(ROPE_BASE)) * 2.0 * index / HD)
    token_pos = jnp.where(lane < HALF, lane + pos[0, 0], lane - HALF + pos[0, HALF])
    angle = token_pos.astype(F32) * inverse
    cos_ref[...] = jnp.cos(angle)
    sin_ref[...] = jnp.sin(angle)

    w_of(4, 3).start()
    acc[...] = jnp.zeros_like(acc)
    accd[...] = jnp.zeros_like(accd)
    tok_copy.wait()
    own_d.wait()

    def arrive(c):
        w_of(0, c).wait_recv()
        for kind in (1, 2, 3, 5):
            w_of(kind, c).start()
        if c == 0:
            d_of(0).wait_recv()
            for kind in (1, 2, 3, 5):
                d_of(kind).start()

    def onward(c):
        for kind in (1, 2, 3):
            w_of(kind, c).wait_recv()
            w_of(5 + kind, c).start()
        if c == 0:
            for kind in (1, 2, 3):
                d_of(kind).wait_recv()
                d_of(5 + kind).start()

    def from_partner(kinds, cs):
        for kind in kinds:
            for c in cs:
                w_of(5 + kind, c).wait_recv()
            if 0 in cs:
                d_of(5 + kind).wait_recv()

    def early(u, carry):
        @pl.when(u == 0)
        def _():
            arrive(0)

        @pl.when(u == 4)
        def _():
            arrive(1)
            onward(0)
            d_of(4).wait_recv()

        for k in range(4):
            @pl.when(u == 4 + k)
            def _():
                w_of(4, k).wait_recv()

        slot = u // 4
        quarter = (col + u % 4) % 4
        base = quarter * 512
        owner = z_hi * 2 + jnp.where(slot == 0, core, 1 - core)
        t = tok[:, pl.ds(pl.multiple_of(owner * ROWS + base, 512), 512)]
        acc[...] += jnp.dot(
            t, wbuf[slot, pl.ds(pl.multiple_of(base, 512), 512), :], preferred_element_type=F32)
        d = dbuf[slot, pl.ds(pl.multiple_of(quarter * 256, 256), 256), :]
        for part in range(2):
            accd[part] += jnp.dot(t[:, part * 256 : part * 256 + 256], d, preferred_element_type=F32)
        return carry

    lax.fori_loop(0, 8, early, 0)
    arrive(2)
    onward(1)

    def late(u, carry):
        @pl.when(u == 4)
        def _():
            from_partner((0, 1, 2, 3), (0, 1))
            arrive(3)

        @pl.when(u == 7)
        def _():
            onward(2)

        @pl.when(u == 9)
        def _():
            from_partner((0,), (2, 3))

        @pl.when(u == 10)
        def _():
            onward(3)

        @pl.when(u == 13)
        def _():
            from_partner((1, 2, 3), (2, 3))

        part = u // 8
        v = u % 8
        slot = jnp.where(part == 0, 2 + v // 4, jnp.where(v < 2, 2 + v, 2 + (v - 2) // 3))
        kind = jnp.where(part == 0, v % 4, jnp.where(v < 2, 0, 1 + (v - 2) % 3))
        moved = jnp.where(kind == 1, 3, jnp.where(kind == 2, 1, jnp.where(kind == 3, 2, 0)))
        quarter = (col + moved) % 4
        base = quarter * 512 + part * 256
        owner = (1 - z_hi) * 2 + jnp.where(slot == 2, core, 1 - core)
        t = tok[:, pl.ds(pl.multiple_of(owner * ROWS + base, 256), 256)]
        acc[...] += jnp.dot(
            t, wbuf[slot, pl.ds(pl.multiple_of(base, 256), 256), :], preferred_element_type=F32)
        accd[part] += jnp.dot(
            t, dbuf[slot, pl.ds(pl.multiple_of(quarter * 256, 256), 256), :], preferred_element_type=F32)
        return carry

    lax.fori_loop(0, 16, late, 0)

    low = (accd[0] + pltpu.roll(accd[1], 64, 1)).astype(BF16)[:, :RANK]
    start0, start1 = pos[0, 0], pos[0, HALF]
    swap = start0 > start1
    lower = jnp.where(swap, start1, start0)
    pair = jnp.where(iota((HD, 2 * HD), 0) == iota((HD, 2 * HD), 1) % HD, 1.0, 0.0).astype(BF16)

    def joined(t):
        cols = slice(t * HD, (t + 1) * HD)
        full = acc[:, cols] + jnp.dot(low, up[:, cols], preferred_element_type=F32)
        high = full.astype(BF16)
        rest = (full - high.astype(F32)).astype(BF16)
        return lax.dot_general(pair, jnp.concatenate([high, rest], axis=1), NT, preferred_element_type=F32)

    def rope(u, k):
        c, n = cos_ref[16 * k : 16 * k + 16, :], sin_ref[16 * k : 16 * k + 16, :]
        return jnp.concatenate([u[:16] * c - u[16:] * n, u[16:] * c + u[:16] * n], axis=0)

    def halves(a, axis):
        lo = lax.slice_in_dim(a, 0, HALF, axis=axis)
        hi = lax.slice_in_dim(a, HALF, TOK, axis=axis)
        return jnp.where(swap, hi, lo), jnp.where(swap, lo, hi)

    ahead = joined(0)
    for j in range(2):
        for k in range(4):
            turned = ahead
            ahead = joined(4 * j + k + 1)
            for t in range(4):
                q = (rope(turned[32 * t : 32 * t + 32], k) * HD ** (-0.5)).astype(BF16).astype(F32) * LOG2E
                cols = slice((4 * j + t) * HALF, (4 * j + t + 1) * HALF)
                for s, part in enumerate(halves(q, 1)):
                    high = part.astype(BF16)
                    q_out[s, 32 * k : 32 * k + 32, cols] = high
                    q_out[s, HD + 32 * k : HD + 32 * k + 32, cols] = (part - high.astype(F32)).astype(BF16)
    both = (ahead, joined(9))
    key = jnp.concatenate(
        [rope(both[k // 2][64 * (k % 2) : 64 * (k % 2) + 32], k) for k in range(4)], axis=0)
    for s, part in enumerate(halves(key.T, 0)):
        kv_out[s, :HALF, :] = part.astype(BF16)
    value = jnp.concatenate(
        [both[k // 2][64 * (k % 2) + 32 : 64 * (k % 2) + 64] for k in range(4)], axis=0).astype(BF16)
    vt = jnp.dot(head_order(), value, preferred_element_type=F32)
    for s, part in enumerate(halves(vt, 1)):
        kv_out[s, HALF : HALF + 128, :] = part[:, :128].astype(BF16)
        kv_out[s, HALF + 128 : HALF + 256, :] = part[:, 128:].astype(BF16)
        kv_out[s, 2 * HALF :, :] = (jnp.zeros((META, HD), F32) + (lower // HALF).astype(F32)).astype(BF16)

    for c in range(4):
        for kind in range(9):
            w_of(kind, c).wait_send()
    for kind in range(9):
        d_of(kind).wait_send()


def project(pos, tokens, codes, scales, down, up):
    view = codes.reshape(4, 8, 160, HD).transpose(0, 2, 1, 3)
    anywhere = pl.BlockSpec(memory_space=pl.ANY)
    vmem = pl.BlockSpec(memory_space=pltpu.VMEM)
    dma = pltpu.SemaphoreType.DMA
    return pl.pallas_call(
        project_kernel,
        out_shape=(
            jax.ShapeDtypeStruct((2, 2 * HD, QH * HALF), BF16),
            jax.ShapeDtypeStruct((2, PIECE, HD), BF16),
        ),
        in_specs=[pl.BlockSpec(memory_space=pltpu.SMEM), anywhere, anywhere, vmem, anywhere, vmem],
        out_specs=(vmem, vmem),
        scratch_shapes=[
            pltpu.VMEM((4, ROWS, OUT), BF16),
            pltpu.VMEM((4, ROWS // 2, HD), BF16),
            pltpu.VMEM((TOK, WIDTH), BF16),
            pltpu.VMEM((TOK, OUT), F32),
            pltpu.VMEM((2, TOK, HD), F32),
            pltpu.VMEM((64, TOK), F32),
            pltpu.VMEM((64, TOK), F32),
            pltpu.VMEM((32, 160, HD), jnp.int32),
            pltpu.VMEM((2, 3, 64, HD), jnp.int32),
            pltpu.VMEM((HEADS, 32, HD), F32),
            pltpu.VMEM((RANK, OUT), BF16),
            dma((2,)), dma((32,)), dma((9, 4)), dma((9, 4)), dma((9,)), dma((9,)),
        ],
        compiler_params=pltpu.CompilerParams(
            collective_id=0, has_side_effects=True, vmem_limit_bytes=60 << 20),
        name="project",
    )(pos, tokens, view, scales, down, up)


ORDER = (
    (0, 0, 0), (0, 1, 0), (0, 3, 0), (0, 0, 1), (0, 0, 3), (1, 0, 0), (0, 2, 0), (0, 0, 2),
    (0, 1, 3), (0, 1, 1), (0, 3, 3), (1, 1, 0), (0, 3, 1), (1, 3, 0), (0, 2, 1), (1, 0, 1),
    (0, 2, 3), (0, 1, 2), (1, 0, 3), (1, 3, 1), (1, 1, 1), (0, 3, 2), (1, 3, 3), (1, 1, 3),
    (1, 2, 0), (1, 2, 1), (0, 2, 2), (1, 0, 2), (1, 2, 3), (1, 3, 2), (1, 1, 2), (1, 2, 2),
)
SLOT = {s: i for i, s in enumerate(ORDER)}
BLOCKS = len(ORDER)
AHEAD = 1


def routes():
    table = {}
    for p in (0, 1):
        table[(0, 1, 0), p] = ("xp", (0, 0, 0))
        table[(0, 3, 0), p] = ("xm", (0, 0, 0))
        for dx in range(4):
            table[(0, dx, 1), p] = ("yp", (0, dx, 0))
            table[(0, dx, 3), p] = ("ym", (0, dx, 0))
        for s in ((0, 0), (1, 0), (3, 0), (2, 0), (0, 1), (0, 3)):
            table[(1,) + s, p] = ("z", (0,) + s)
        for dy in (1, 2, 3):
            table[(1, 1, dy), p] = ("xp", (1, 0, dy))
            table[(1, 3, dy), p] = ("xm", (1, 0, dy))
    table[(0, 2, 0), 0] = ("xm", (0, 3, 0))
    table[(0, 2, 0), 1] = ("xp", (0, 1, 0))
    for dx in range(4):
        table[(0, dx, 2), 0] = ("ym", (0, dx, 3))
        table[(0, dx, 2), 1] = ("yp", (0, dx, 1))
    table[(1, 0, 2), 0] = ("ym", (1, 0, 3))
    table[(1, 0, 2), 1] = ("yp", (1, 0, 1))
    for dy in (1, 2, 3):
        table[(1, 2, dy), 0] = ("xm", (1, 3, dy))
        table[(1, 2, dy), 1] = ("xp", (1, 1, dy))
    return table


def forwards():
    opposite = {"xp": "xm", "xm": "xp", "yp": "ym", "ym": "yp", "z": "z"}
    table = {i: [] for i in range(BLOCKS)}
    for (s, p), (origin, source) in routes().items():
        table[SLOT[source]].append((SLOT[s], p, opposite[origin]))
    return {i: sorted(v) for i, v in table.items()}


def attend_kernel(pos, q, kv, out, kvbuf, k2, vt1, vt2, m_ref, acc, local, send, recv):
    z_hi, core, z_lo, x, y = place()
    peers = {
        "xp": device(z_hi, core, z_lo, x + 1, y), "xm": device(z_hi, core, z_lo, x + 3, y),
        "yp": device(z_hi, core, z_lo, x, y + 1), "ym": device(z_hi, core, z_lo, x, y + 3),
        "z": device(z_hi, core, 1 - z_lo, x, y),
    }
    table = forwards()
    own = pltpu.make_async_copy(kv, kvbuf.at[0], local.at[0])
    own.start()
    barrier = pltpu.get_barrier_semaphore()
    for peer in peers.values():
        pl.semaphore_signal(barrier, inc=1, device_id=peer, device_id_type=MESH)
    pl.semaphore_wait(barrier, len(peers))
    own.wait()

    def copy(source, slot, piece, peer):
        return pltpu.make_async_remote_copy(
            src_ref=kvbuf.at[source, piece], dst_ref=kvbuf.at[slot, piece],
            send_sem=send.at[slot, piece], recv_sem=recv.at[slot, piece],
            device_id=peer, device_id_type=MESH,
        )

    def forward(source):
        for slot, piece, to in table[source]:
            copy(source, slot, piece, peers[to]).start()

    def take(slot):
        for piece in range(2):
            copy(0, slot, piece, peers["z"]).wait_recv()

    forward(0)

    start0, start1 = pos[0, 0], pos[0, HALF]
    swap = start0 > start1
    mine = (jnp.where(swap, start1, start0) // HALF).astype(F32)
    one = jnp.ones((META, HALF), BF16)
    vt1[HD:, :HALF] = one
    vt2[HD:, :] = one

    def keys(slot, piece):
        return kvbuf[slot, piece, :HALF, :]

    def values(slot, piece):
        return jnp.concatenate(
            [kvbuf[slot, piece, HALF : HALF + 128, :], kvbuf[slot, piece, HALF + 128 : HALF + 256, :]], axis=1)

    def scores(k, qt):
        return jnp.dot(jnp.concatenate([k, k], axis=1), qt, preferred_element_type=F32)

    def weigh(vt, s, m):
        return jnp.dot(vt, jnp.exp2(s - m).astype(BF16), preferred_element_type=F32)

    def top(s):
        return jnp.max(s, axis=0, keepdims=True)

    vt1[:HD, :HALF] = values(0, 0)
    vt2[:HD, :] = values(0, 1)
    k2[...] = keys(0, 1)

    def own_head(h, carry):
        cols = pl.ds(pl.multiple_of(h * HALF, HALF), HALF)
        q0, q1 = q[0, :, cols], q[1, :, cols]
        seen = iota((HALF, HALF), 0) <= iota((HALF, HALF), 1)
        s00 = jnp.where(seen, scores(keys(0, 0), q0), -jnp.inf)
        m0 = top(s00)
        m_ref[0, h] = jnp.broadcast_to(m0, (8, HALF))
        acc[0, h] = weigh(vt1[:, :HALF], s00, m0)
        s10 = scores(keys(0, 0), q1)
        s11 = jnp.where(seen, scores(k2[...], q1), -jnp.inf)
        m1 = jnp.maximum(top(s10), top(s11))
        m_ref[1, h] = jnp.broadcast_to(m1, (8, HALF))
        acc[1, h] = weigh(vt1[:, :HALF], s10, m1) + weigh(vt2[...], s11, m1)
        return carry

    lax.fori_loop(0, QH, own_head, 0, unroll=2)

    def step(i, carry):
        def come(k):
            @pl.when(i + AHEAD == k)
            def _():
                take(k)
                forward(k)

        for group in range(0, BLOCKS, 6):
            @pl.when((i + AHEAD >= group) & (i + AHEAD < group + 6))
            def _():
                for k in range(max(group, 1), min(group + 6, BLOCKS)):
                    come(k)

        @pl.when(i > 0)
        def _():
            theirs = jnp.max(kvbuf[i, 0, 2 * HALF :, :].astype(F32))
            c = theirs < mine
            lo_bias = jnp.where(c, 0.0, NEG)
            hi_bias = jnp.where(c, NEG, 0.0)
            w_lo = jnp.where(c, 1.0, 0.0)
            w_hi = jnp.where(c, 0.0, 1.0)
            k2[...] = jnp.where(c, keys(i, 0), keys(i, 1))
            vt1[:HD, :HALF] = values(i, 0)
            low_v, zero = values(i, 0), jnp.zeros((HD, HALF), BF16)
            vt1[:HD, HALF:] = jnp.where(c, zero, values(i, 1))
            vt1[HD:, HALF:] = jnp.where(c, zero[:META], one)
            vt2[:HD, :] = jnp.where(c, low_v, zero)
            vt2[HD:, :] = jnp.where(c, one, zero[:META])

            def product(h):
                cols = slice(h * HALF, (h + 1) * HALF)
                q1 = q[1, :, cols]
                q2 = jnp.where(c, q[0, :, cols], q1)
                return scores(keys(i, 0), q1), scores(k2[...], q2)

            def soften(h, s1, s2):
                t1, t2 = top(s1), top(s2)
                m_lo, m_hi = m_ref[0, h, :1, :], m_ref[1, h, :1, :]
                n_lo = jnp.maximum(m_lo, t2 + lo_bias)
                n_hi = jnp.maximum(m_hi, jnp.maximum(t1, t2 + hi_bias))
                e1 = jnp.exp2(s1 - n_hi).astype(BF16)
                e2 = jnp.exp2(s2 - jnp.where(c, n_lo, n_hi)).astype(BF16)
                m_ref[0, h] = jnp.broadcast_to(n_lo, (8, HALF))
                m_ref[1, h] = jnp.broadcast_to(n_hi, (8, HALF))
                return e1, e2, jnp.exp2(m_lo - n_lo), jnp.exp2(m_hi - n_hi)

            def gather(h, e1, e2, f_lo, f_hi):
                o_hi = jnp.dot(vt1[...], jnp.concatenate([e1, e2], axis=0), preferred_element_type=F32)
                o_lo = jnp.dot(vt2[...], e2, preferred_element_type=F32)
                acc[0, h] = acc[0, h] * f_lo + o_lo
                acc[1, h] = acc[1, h] * f_hi + o_hi

            ahead, ready = product(0), None
            for h in range(QH):
                now = ahead
                if h + 1 < QH:
                    ahead = product(h + 1)
                if ready is not None:
                    gather(h - 1, *ready)
                ready = soften(h, *now)
            gather(QH - 1, *ready)

        return carry

    lax.fori_loop(1 - AHEAD, BLOCKS, step, 0)

    for h in range(QH):
        cols = slice(h * HD, (h + 1) * HD)
        parts = []
        for s in range(2):
            total = acc[s, h, HD : HD + 1, :]
            parts.append((acc[s, h, :HD, :] / total).T)
        out[:HALF, cols] = jnp.where(swap, parts[1], parts[0]).astype(BF16)
        out[HALF:, cols] = jnp.where(swap, parts[0], parts[1]).astype(BF16)

    def drain(slot, carry):
        for piece in range(2):
            copy(0, slot, piece, peers["z"]).wait_send()
        return carry

    lax.fori_loop(1, BLOCKS, drain, 0)


def attend(pos, q, kv):
    anywhere = pl.BlockSpec(memory_space=pl.ANY)
    vmem = pl.BlockSpec(memory_space=pltpu.VMEM)
    dma = pltpu.SemaphoreType.DMA
    return pl.pallas_call(
        attend_kernel,
        out_shape=jax.ShapeDtypeStruct((TOK, QH * HD), BF16),
        in_specs=[pl.BlockSpec(memory_space=pltpu.SMEM), vmem, anywhere],
        out_specs=vmem,
        scratch_shapes=[
            pltpu.VMEM((BLOCKS, 2, PIECE, HD), BF16),
            pltpu.VMEM((HALF, HD), BF16),
            pltpu.VMEM((HD + META, 2 * HALF), BF16),
            pltpu.VMEM((HD + META, HALF), BF16),
            pltpu.VMEM((2, QH, 8, HALF), F32),
            pltpu.VMEM((2, QH, HD + META, HALF), F32),
            dma((1,)), dma((BLOCKS, 2)), dma((BLOCKS, 2)),
        ],
        compiler_params=pltpu.CompilerParams(
            collective_id=1, has_side_effects=True, vmem_limit_bytes=60 << 20),
        name="attend",
    )(pos, q, kv)


def on_device(tokens, codes, scales, down_adapter_matrix, up_adapter_matrix, positions):
    down = down_adapter_matrix.reshape(4, 2, HALF, RANK).transpose(0, 2, 1, 3).reshape(ROWS // 2, HD)
    q, kv = project(positions, tokens[0], codes, scales, down, up_adapter_matrix)
    return attend(positions, q, kv)[None]


def solution(mesh):
    return jax.shard_map(
        on_device,
        mesh=mesh,
        in_specs=(
            P("fsdp", "ctx", None), P("fsdp", None), P("fsdp", None), P("fsdp", None), P(), P("fsdp", "ctx"),
        ),
        out_specs=P("fsdp", "ctx", None),
        check_vma=False,
    )
```

```python
import jax
import jax.numpy as jnp
from jax import lax
from jax.experimental import pallas as pl
from jax.experimental.pallas import tpu as pltpu
from jax.sharding import PartitionSpec as P

MESH = pl.DeviceIdType.MESH
QH = 8
HD = 128
HEADS = QH + 2
HALF = 256
TOK = 512
WIDTH = 8192
OUT = 1280
ROWS = 2048
CHUNK = 64
RANK = 64
META = 16
PIECE = 512 + META
ROPE_BASE = 500000.0
LEVELS = (
    -1.0, -0.6961928009986877, -0.5250730514526367, -0.39491748809814453,
    -0.28444138169288635, -0.18477343022823334, -0.09105003625154495, 0.0,
    0.07958029955625534, 0.16093020141124725, 0.24611230194568634, 0.33791524171829224,
    0.44070982933044434, 0.5626170039176941, 0.7229568362236023, 1.0,
)
F32 = jnp.float32
BF16 = jnp.bfloat16
NT = (((1,), (1,)), ((), ()))
NEG = -1e30
LOG2E = 1.4426950408889634


def iota(shape, dim):
    return lax.broadcasted_iota(jnp.int32, shape, dim)


def head_order():
    p = iota((HD, HD), 1)
    return jnp.where(iota((HD, HD), 0) == 4 * (p % 32) + p // 32, 1.0, 0.0).astype(BF16)


def plane(t):
    depth = 512 if t < 8 else 256
    lane = iota((depth, HD), 1)
    column = 4 * lane + t % 4 if t < 8 else 4 * (lane % 64) + 2 * (t - 8) + lane // 64
    return (t // 4) * 512, jnp.where(iota((depth, HD), 0) == column, 1.0, 0.0).astype(BF16)


def lookup(tables, words, move):
    numbers = lax.GatherDimensionNumbers(
        offset_dims=(), collapsed_slice_dims=(0,), start_index_map=(0,),
        operand_batching_dims=(1,), start_indices_batching_dims=(1,))
    index = (words >> move) & 7
    low, high = (
        lax.gather(t, index[..., None], numbers, slice_sizes=(1, 1), mode=lax.GatherScatterMode.PROMISE_IN_BOUNDS)
        for t in tables)
    return jnp.where((words & (8 << move)) != 0, high, low)


def place():
    f, c = lax.axis_index("fsdp"), lax.axis_index("ctx")
    return f // 2, f % 2, c // 16, (c // 4) % 4, c % 4


def device(z_hi, core, z_lo, x, y):
    return (z_hi * 2 + core, z_lo * 16 + (x % 4) * 4 + y % 4)


def project_kernel(
    pos, tok_hbm, codes, scales, d_hbm, up_in, q_out, kv_out,
    wbuf, dbuf, tok, acc, accd, cos_ref, sin_ref, raw, nat, sc, up,
    local, fetched, wsend, wrecv, dsend, drecv,
):
    z_hi, core, z_lo, x, y = place()
    z = z_hi * 2 + z_lo
    cross_z = jnp.where(z % 2 == 0, (z + 3) % 4, (z + 1) % 4)
    cross = device(cross_z // 2, core, cross_z % 2, x, y)
    partner = device(z_hi, 1 - core, z_lo, x, y)
    xp, xm = device(z_hi, core, z_lo, x + 1, y), device(z_hi, core, z_lo, x + 3, y)
    yp, ym = device(z_hi, core, z_lo, x, y + 1), device(z_hi, core, z_lo, x, y + 3)
    col = (x + 2 * y) % 4

    def block(n):
        return (col * 8 + n) % 32

    def fetch(n):
        rows = pl.ds(pl.multiple_of((col + n) % 4 * 1280, 1280), 1280)
        return pltpu.make_async_copy(codes.at[rows, :], raw.at[rows, :], fetched.at[n])

    for n in range(4):
        fetch(n).start()
    tok_copy = pltpu.make_async_copy(tok_hbm, tok, local.at[0])
    own_d = pltpu.make_async_copy(d_hbm, dbuf.at[0], local.at[1])
    own_d.start()
    tok_copy.start()

    barrier = pltpu.get_barrier_semaphore()
    for peer in (cross, partner, xp, xm, yp, ym):
        pl.semaphore_signal(barrier, inc=1, device_id=peer, device_id_type=MESH)

    for t in range(HEADS):
        first, picks = plane(t)
        cols = slice(first, first + picks.shape[0])
        sc[t] = jnp.dot(scales[:, cols], picks, preferred_element_type=F32)
        half_up = 0.5 * jnp.dot(up_in[:, cols], picks, preferred_element_type=F32)
        up[:, t * HD : (t + 1) * HD] = half_up.astype(BF16)
    pl.semaphore_wait(barrier, 6)

    shift = (0, 3, 1, 2)

    def rows_of(k, c):
        quarter = (col + shift[k]) % 4
        return pl.ds(pl.multiple_of(quarter * 512 + c * CHUNK, CHUNK), CHUNK)

    def drows_of(k):
        quarter = (col + shift[k]) % 4
        return pl.ds(pl.multiple_of(quarter * 256, 256), 256)

    def wcopy(kind, c, src, dst, peer):
        return pltpu.make_async_remote_copy(
            src_ref=src, dst_ref=dst, send_sem=wsend.at[kind, c], recv_sem=wrecv.at[kind, c],
            device_id=peer, device_id_type=MESH,
        )

    def dcopy(kind, src, dst, peer):
        return pltpu.make_async_remote_copy(
            src_ref=src, dst_ref=dst, send_sem=dsend.at[kind], recv_sem=drecv.at[kind],
            device_id=peer, device_id_type=MESH,
        )

    def w_of(kind, c):
        if kind == 0:
            rows = rows_of(0, c)
            return wcopy(0, c, wbuf.at[0, rows, :], wbuf.at[2, rows, :], cross)
        if kind in (1, 2, 3):
            rows = rows_of(0, c)
            peer = xp if kind == 1 else xm if kind == 2 else (yp, ym)[c % 2]
            return wcopy(kind, c, wbuf.at[2, rows, :], wbuf.at[2, rows, :], peer)
        if kind == 4:
            rows = pl.ds(pl.multiple_of((col + c) % 4 * 512, 512), 512)
            return wcopy(4, c, wbuf.at[0, rows, :], wbuf.at[1, rows, :], partner)
        rows = rows_of(kind - 5, c)
        return wcopy(kind, c, wbuf.at[2, rows, :], wbuf.at[3, rows, :], partner)

    def d_of(kind):
        if kind == 0:
            rows = drows_of(0)
            return dcopy(0, d_hbm.at[rows, :], dbuf.at[2, rows, :], cross)
        if kind in (1, 2, 3):
            rows = drows_of(0)
            return dcopy(kind, dbuf.at[2, rows, :], dbuf.at[2, rows, :], (xp, xm, yp)[kind - 1])
        if kind == 4:
            return dcopy(4, d_hbm, dbuf.at[1], partner)
        rows = drows_of(kind - 5)
        return dcopy(kind, dbuf.at[2, rows, :], dbuf.at[3, rows, :], partner)

    d_of(0).start()
    d_of(4).start()

    left = iota((8, HD), 1) < 64
    place_in = iota((64, HD), 1)
    digit = 4 * (place_in // 64)
    tables = []
    for first in (0, 8):
        table = jnp.zeros((8, HD), F32)
        for n in range(8):
            table = jnp.where(iota((8, HD), 0) == n, LEVELS[first + n], table)
        tables.append(table)

    def dequantize(n, slot):
        b = block(n)
        for g in range(4):
            u = [raw[pl.ds(b // 8 * 1280 + 8 * (40 * g + i) + b % 8, 8, stride=40), :] for i in range(5)]
            r2, r3, r4 = (pltpu.roll(u[i], 64, 1) for i in (2, 3, 4))
            odd = (jnp.where(left, r2, r3), jnp.where(left, r3, r4), r4)
            for j in range(3):
                nat[slot, j, pl.ds(16 * g, 8, stride=2), :] = u[j]
                nat[slot, j, pl.ds(16 * g + 1, 8, stride=2), :] = odd[j]

    def levels(n, slot):
        b = block(n)
        rows = pl.ds(pl.multiple_of(b * 64, 64), 64)
        for t in range(HEADS):
            words = nat[slot, t // 4]
            if t < 8:
                move = 4 * (t % 4)
            else:
                words = jnp.where(place_in < 64, words, pltpu.roll(words, 64, 1))
                move = digit + 8 * (t - 8)
            level = jnp.concatenate(
                [lookup(tables, words[r : r + 8], move if t < 8 else move[:8]) for r in range(0, 64, 8)], axis=0)
            wbuf[0, rows, t * HD : (t + 1) * HD] = (level * sc[t, pl.ds(b, 1), :]).astype(BF16)

    def arrive(c):
        w_of(0, c).wait_recv()
        for kind in (1, 2, 3, 5):
            w_of(kind, c).start()
        if c == 0:
            d_of(0).wait_recv()
            for kind in (1, 2, 3, 5):
                d_of(kind).start()

    def onward(c):
        for kind in (1, 2, 3):
            w_of(kind, c).wait_recv()
            w_of(5 + kind, c).start()
        if c == 0:
            for kind in (1, 2, 3):
                d_of(kind).wait_recv()
                d_of(5 + kind).start()

    def from_partner(kinds, cs):
        for kind in kinds:
            for c in cs:
                w_of(5 + kind, c).wait_recv()
            if 0 in cs:
                d_of(5 + kind).wait_recv()

    def pair(n, carry):
        for k in range(4):
            @pl.when(n == 4 * k)
            def _():
                fetch(k).wait()

        dequantize(2 * n, 0)
        dequantize(2 * n + 1, 1)
        levels(2 * n, 0)
        levels(2 * n + 1, 1)

        @pl.when(n <= 4)
        def _():
            for c in range(4):
                @pl.when(n == c + 1)
                def _():
                    w_of(0, 2 * c).start()
                    w_of(0, 2 * c + 1).start()

        @pl.when(n == 10)
        def _():
            arrive(0)

        @pl.when((n > 0) & (n % 4 == 0))
        def _():
            for c in range(3):
                @pl.when(n == 4 * c + 4)
                def _():
                    w_of(4, c).start()

        return carry

    lax.fori_loop(0, 16, pair, 0)

    row = iota((64, TOK), 0)
    lane = iota((64, TOK), 1)
    index = (4 * (row % 16) + row // 16).astype(F32)
    inverse = jnp.exp(-jnp.log(F32(ROPE_BASE)) * 2.0 * index / HD)
    token_pos = jnp.where(lane < HALF, lane + pos[0, 0], lane - HALF + pos[0, HALF])
    angle = token_pos.astype(F32) * inverse
    cos_ref[...] = jnp.cos(angle)
    sin_ref[...] = jnp.sin(angle)

    w_of(4, 3).start()
    acc[...] = jnp.zeros_like(acc)
    accd[...] = jnp.zeros_like(accd)
    tok_copy.wait()
    own_d.wait()

    def early(u, carry):
        @pl.when(u == 0)
        def _():
            arrive(1)

        @pl.when(u == 2)
        def _():
            onward(0)
            arrive(2)

        @pl.when(u == 4)
        def _():
            onward(1)
            arrive(3)
            d_of(4).wait_recv()

        @pl.when(u == 7)
        def _():
            onward(2)
            arrive(4)

        for k in range(4):
            @pl.when(u == 4 + k)
            def _():
                w_of(4, k).wait_recv()

        slot = u // 4
        quarter = (col + u % 4) % 4
        base = quarter * 512
        owner = z_hi * 2 + jnp.where(slot == 0, core, 1 - core)
        t = tok[:, pl.ds(pl.multiple_of(owner * ROWS + base, 512), 512)]
        acc[...] += jnp.dot(
            t, wbuf[slot, pl.ds(pl.multiple_of(base, 512), 512), :], preferred_element_type=F32)
        d = dbuf[slot, pl.ds(pl.multiple_of(quarter * 256, 256), 256), :]
        for part in range(2):
            accd[part] += jnp.dot(t[:, part * 256 : part * 256 + 256], d, preferred_element_type=F32)
        return carry

    lax.fori_loop(0, 8, early, 0)

    def source(slot, kind):
        moved = jnp.where(kind == 1, 3, jnp.where(kind == 2, 1, jnp.where(kind == 3, 2, 0)))
        return (col + moved) % 4, (1 - z_hi) * 2 + jnp.where(slot == 2, core, 1 - core)

    def late(u, carry):
        @pl.when(u == 1)
        def _():
            from_partner((0,), (0, 1, 2, 3))

        @pl.when(u == 2)
        def _():
            onward(3)
            arrive(5)

        @pl.when(u == 5)
        def _():
            from_partner((1, 2, 3), (0, 1, 2, 3))

        @pl.when(u == 6)
        def _():
            onward(4)
            arrive(6)

        @pl.when(u == 8)
        def _():
            onward(5)
            arrive(7)

        @pl.when(u == 9)
        def _():
            from_partner((0,), (4, 5, 6, 7))

        part = u // 8
        v = u % 8
        slot = jnp.where(v < 2, 2 + v, 2 + (v - 2) // 3)
        kind = jnp.where(v < 2, 0, 1 + (v - 2) % 3)
        quarter, owner = source(slot, kind)
        base = quarter * 512 + part * 256
        t = tok[:, pl.ds(pl.multiple_of(owner * ROWS + base, 256), 256)]
        acc[...] += jnp.dot(
            t, wbuf[slot, pl.ds(pl.multiple_of(base, 256), 256), :], preferred_element_type=F32)
        accd[part] += jnp.dot(
            t, dbuf[slot, pl.ds(pl.multiple_of(quarter * 256, 256), 256), :], preferred_element_type=F32)
        return carry

    lax.fori_loop(0, 10, late, 0)

    def last(u, carry):
        @pl.when(u == 1)
        def _():
            from_partner((1, 2, 3), (4, 5))
            onward(6)

        @pl.when(u == 3)
        def _():
            onward(7)

        @pl.when(u == 4)
        def _():
            from_partner((1, 2, 3), (6, 7))

        part = u // 3
        ts, ws, ds = [], [], []
        for n in range(2):
            i = 2 * (u % 3) + n
            slot = 2 + i // 3
            quarter, owner = source(slot, 1 + i % 3)
            base = quarter * 512 + 256 + part * 128
            ts.append(tok[:, pl.ds(pl.multiple_of(owner * ROWS + base, 128), 128)])
            ws.append(wbuf[slot, pl.ds(pl.multiple_of(base, 128), 128), :])
            ds.append(dbuf[slot, pl.ds(pl.multiple_of(quarter * 256 + part * 128, 128), 128), :])
        t = jnp.concatenate(ts, axis=1)
        acc[...] += jnp.dot(t, jnp.concatenate(ws, axis=0), preferred_element_type=F32)
        accd[1] += jnp.dot(t, jnp.concatenate(ds, axis=0), preferred_element_type=F32)
        return carry

    lax.fori_loop(0, 6, last, 0)

    low = (accd[0] + pltpu.roll(accd[1], 64, 1)).astype(BF16)[:, :RANK]
    start0, start1 = pos[0, 0], pos[0, HALF]
    swap = start0 > start1
    lower = jnp.where(swap, start1, start0)
    pair = jnp.where(iota((HD, 2 * HD), 0) == iota((HD, 2 * HD), 1) % HD, 1.0, 0.0).astype(BF16)

    def joined(t):
        cols = slice(t * HD, (t + 1) * HD)
        full = acc[:, cols] + jnp.dot(low, up[:, cols], preferred_element_type=F32)
        high = full.astype(BF16)
        rest = (full - high.astype(F32)).astype(BF16)
        return lax.dot_general(pair, jnp.concatenate([high, rest], axis=1), NT, preferred_element_type=F32)

    def rope(u, k):
        c, n = cos_ref[16 * k : 16 * k + 16, :], sin_ref[16 * k : 16 * k + 16, :]
        return jnp.concatenate([u[:16] * c - u[16:] * n, u[16:] * c + u[:16] * n], axis=0)

    def halves(a, axis):
        lo = lax.slice_in_dim(a, 0, HALF, axis=axis)
        hi = lax.slice_in_dim(a, HALF, TOK, axis=axis)
        return jnp.where(swap, hi, lo), jnp.where(swap, lo, hi)

    ahead = joined(0)
    for j in range(2):
        for k in range(4):
            turned = ahead
            ahead = joined(4 * j + k + 1)
            for t in range(4):
                q = (rope(turned[32 * t : 32 * t + 32], k) * HD ** (-0.5)).astype(BF16).astype(F32) * LOG2E
                for s, part in enumerate(halves(q, 1)):
                    high = part.astype(BF16)
                    rest = (part - high.astype(F32)).astype(BF16)
                    for n in range(2):
                        tile = 2 * (4 * j + t) + n
                        q_out[s, tile, 32 * k : 32 * k + 32, :] = high[:, n * 128 : n * 128 + 128]
                        q_out[s, tile, HD + 32 * k : HD + 32 * k + 32, :] = rest[:, n * 128 : n * 128 + 128]
    both = (ahead, joined(9))
    key = jnp.concatenate(
        [rope(both[k // 2][64 * (k % 2) : 64 * (k % 2) + 32], k) for k in range(4)], axis=0)
    for s, part in enumerate(halves(key.T, 0)):
        kv_out[s, :HALF, :] = part.astype(BF16)
    value = jnp.concatenate(
        [both[k // 2][64 * (k % 2) + 32 : 64 * (k % 2) + 64] for k in range(4)], axis=0).astype(BF16)
    vt = jnp.dot(head_order(), value, preferred_element_type=F32)
    for s, part in enumerate(halves(vt, 1)):
        kv_out[s, HALF : HALF + 128, :] = part[:, :128].astype(BF16)
        kv_out[s, HALF + 128 : HALF + 256, :] = part[:, 128:].astype(BF16)
        kv_out[s, 2 * HALF :, :] = (jnp.zeros((META, HD), F32) + (lower // HALF).astype(F32)).astype(BF16)

    for kind in range(9):
        for c in range(4 if kind == 4 else 8):
            w_of(kind, c).wait_send()
    for kind in range(9):
        d_of(kind).wait_send()


def project(pos, tokens, codes, scales, down, up):
    view = codes.reshape(4, 8, 160, HD).transpose(0, 2, 1, 3).reshape(5120, HD)
    anywhere = pl.BlockSpec(memory_space=pl.ANY)
    vmem = pl.BlockSpec(memory_space=pltpu.VMEM)
    dma = pltpu.SemaphoreType.DMA
    return pl.pallas_call(
        project_kernel,
        out_shape=(
            jax.ShapeDtypeStruct((2, 2 * QH, 2 * HD, 128), BF16),
            jax.ShapeDtypeStruct((2, PIECE, HD), BF16),
        ),
        in_specs=[pl.BlockSpec(memory_space=pltpu.SMEM), anywhere, anywhere, vmem, anywhere, vmem],
        out_specs=(vmem, vmem),
        scratch_shapes=[
            pltpu.VMEM((4, ROWS, OUT), BF16),
            pltpu.VMEM((4, ROWS // 2, HD), BF16),
            pltpu.VMEM((TOK, WIDTH), BF16),
            pltpu.VMEM((TOK, OUT), F32),
            pltpu.VMEM((2, TOK, HD), F32),
            pltpu.VMEM((64, TOK), F32),
            pltpu.VMEM((64, TOK), F32),
            pltpu.VMEM((5120, HD), jnp.int32),
            pltpu.VMEM((2, 3, 64, HD), jnp.int32),
            pltpu.VMEM((HEADS, 32, HD), F32),
            pltpu.VMEM((RANK, OUT), BF16),
            dma((2,)), dma((4,)), dma((9, 8)), dma((9, 8)), dma((9,)), dma((9,)),
        ],
        compiler_params=pltpu.CompilerParams(
            collective_id=0, has_side_effects=True, vmem_limit_bytes=60 << 20),
        name="project",
    )(pos, tokens, view, scales, down, up)


ORDER = (
    (0, 0, 0), (0, 1, 0), (0, 3, 0), (0, 0, 1), (0, 0, 3), (1, 0, 0), (0, 2, 0), (0, 0, 2),
    (0, 1, 3), (0, 1, 1), (0, 3, 3), (1, 1, 0), (0, 3, 1), (1, 3, 0), (0, 2, 1), (1, 0, 1),
    (0, 2, 3), (0, 1, 2), (1, 0, 3), (1, 3, 1), (1, 1, 1), (0, 3, 2), (1, 3, 3), (1, 1, 3),
    (1, 2, 0), (1, 2, 1), (0, 2, 2), (1, 0, 2), (1, 2, 3), (1, 3, 2), (1, 1, 2), (1, 2, 2),
)
SLOT = {s: i for i, s in enumerate(ORDER)}
BLOCKS = len(ORDER)
AHEAD = 1


def routes():
    table = {}
    for p in (0, 1):
        table[(0, 1, 0), p] = ("xp", (0, 0, 0))
        table[(0, 3, 0), p] = ("xm", (0, 0, 0))
        for dx in range(4):
            table[(0, dx, 1), p] = ("yp", (0, dx, 0))
            table[(0, dx, 3), p] = ("ym", (0, dx, 0))
        for s in ((0, 0), (1, 0), (3, 0), (2, 0), (0, 1), (0, 3)):
            table[(1,) + s, p] = ("z", (0,) + s)
        for dy in (1, 2, 3):
            table[(1, 1, dy), p] = ("xp", (1, 0, dy))
            table[(1, 3, dy), p] = ("xm", (1, 0, dy))
    table[(0, 2, 0), 0] = ("xm", (0, 3, 0))
    table[(0, 2, 0), 1] = ("xp", (0, 1, 0))
    for dx in range(4):
        table[(0, dx, 2), 0] = ("ym", (0, dx, 3))
        table[(0, dx, 2), 1] = ("yp", (0, dx, 1))
    table[(1, 0, 2), 0] = ("ym", (1, 0, 3))
    table[(1, 0, 2), 1] = ("yp", (1, 0, 1))
    for dy in (1, 2, 3):
        table[(1, 2, dy), 0] = ("xm", (1, 3, dy))
        table[(1, 2, dy), 1] = ("xp", (1, 1, dy))
    return table


def forwards():
    opposite = {"xp": "xm", "xm": "xp", "yp": "ym", "ym": "yp", "z": "z"}
    table = {i: [] for i in range(BLOCKS)}
    for (s, p), (origin, source) in routes().items():
        table[SLOT[source]].append((SLOT[s], p, opposite[origin]))
    return {i: sorted(v) for i, v in table.items()}


def attend_kernel(pos, q_in, kv, out, kvbuf, q, k2, vt1, vt2, m_ref, acc, local, send, recv):
    z_hi, core, z_lo, x, y = place()
    peers = {
        "xp": device(z_hi, core, z_lo, x + 1, y), "xm": device(z_hi, core, z_lo, x + 3, y),
        "yp": device(z_hi, core, z_lo, x, y + 1), "ym": device(z_hi, core, z_lo, x, y + 3),
        "z": device(z_hi, core, 1 - z_lo, x, y),
    }
    table = forwards()
    own = pltpu.make_async_copy(kv, kvbuf.at[0], local.at[0])
    own_q = pltpu.make_async_copy(q_in, q, local.at[1])
    own.start()
    own_q.start()
    barrier = pltpu.get_barrier_semaphore()
    for peer in peers.values():
        pl.semaphore_signal(barrier, inc=1, device_id=peer, device_id_type=MESH)
    pl.semaphore_wait(barrier, len(peers))
    own.wait()

    def copy(source, slot, piece, peer):
        return pltpu.make_async_remote_copy(
            src_ref=kvbuf.at[source, piece], dst_ref=kvbuf.at[slot, piece],
            send_sem=send.at[slot, piece], recv_sem=recv.at[slot, piece],
            device_id=peer, device_id_type=MESH,
        )

    def forward(source):
        for slot, piece, to in table[source]:
            copy(source, slot, piece, peers[to]).start()

    def take(slot):
        for piece in range(2):
            copy(0, slot, piece, peers["z"]).wait_recv()

    forward(0)

    start0, start1 = pos[0, 0], pos[0, HALF]
    swap = start0 > start1
    mine = (jnp.where(swap, start1, start0) // HALF).astype(F32)
    one = jnp.ones((META, HALF), BF16)
    vt1[HD:, :HALF] = one
    vt2[HD:, :] = one

    def query(s, h):
        return jnp.concatenate([q[s, 2 * h], q[s, 2 * h + 1]], axis=1)

    def keys(slot, piece):
        return kvbuf[slot, piece, :HALF, :]

    def values(slot, piece):
        return jnp.concatenate(
            [kvbuf[slot, piece, HALF : HALF + 128, :], kvbuf[slot, piece, HALF + 128 : HALF + 256, :]], axis=1)

    def scores(k, qt):
        return jnp.dot(jnp.concatenate([k, k], axis=1), qt, preferred_element_type=F32)

    def weigh(vt, s, m):
        return jnp.dot(vt, jnp.exp2(s - m).astype(BF16), preferred_element_type=F32)

    def top(s):
        return jnp.max(s, axis=0, keepdims=True)

    own_q.wait()
    vt1[:HD, :HALF] = values(0, 0)
    vt2[:HD, :] = values(0, 1)
    k2[...] = keys(0, 1)

    def own_head(h, carry):
        q0, q1 = query(0, h), query(1, h)
        seen = iota((HALF, HALF), 0) <= iota((HALF, HALF), 1)
        s00 = jnp.where(seen, scores(keys(0, 0), q0), -jnp.inf)
        m0 = top(s00)
        m_ref[0, h] = jnp.broadcast_to(m0, (8, HALF))
        acc[0, h] = weigh(vt1[:, :HALF], s00, m0)
        s10 = scores(keys(0, 0), q1)
        s11 = jnp.where(seen, scores(k2[...], q1), -jnp.inf)
        m1 = jnp.maximum(top(s10), top(s11))
        m_ref[1, h] = jnp.broadcast_to(m1, (8, HALF))
        acc[1, h] = weigh(vt1[:, :HALF], s10, m1) + weigh(vt2[...], s11, m1)
        return carry

    lax.fori_loop(0, QH, own_head, 0, unroll=2)

    def step(i, carry):
        def come(k):
            @pl.when(i + AHEAD == k)
            def _():
                take(k)
                forward(k)

        for group in range(0, BLOCKS, 6):
            @pl.when((i + AHEAD >= group) & (i + AHEAD < group + 6))
            def _():
                for k in range(max(group, 1), min(group + 6, BLOCKS)):
                    come(k)

        @pl.when(i > 0)
        def _():
            theirs = jnp.max(kvbuf[i, 0, 2 * HALF :, :].astype(F32))
            c = theirs < mine
            lo_bias = jnp.where(c, 0.0, NEG)
            hi_bias = jnp.where(c, NEG, 0.0)
            w_lo = jnp.where(c, 1.0, 0.0)
            w_hi = jnp.where(c, 0.0, 1.0)
            k2[...] = jnp.where(c, keys(i, 0), keys(i, 1))
            vt1[:HD, :HALF] = values(i, 0)
            low_v, zero = values(i, 0), jnp.zeros((HD, HALF), BF16)
            vt1[:HD, HALF:] = jnp.where(c, zero, values(i, 1))
            vt1[HD:, HALF:] = jnp.where(c, zero[:META], one)
            vt2[:HD, :] = jnp.where(c, low_v, zero)
            vt2[HD:, :] = jnp.where(c, one, zero[:META])

            def product(h):
                q1 = query(1, h)
                q2 = jnp.where(c, query(0, h), q1)
                return scores(keys(i, 0), q1), scores(k2[...], q2)

            def soften(h, s1, s2):
                t1, t2 = top(s1), top(s2)
                m_lo, m_hi = m_ref[0, h, :1, :], m_ref[1, h, :1, :]
                n_lo = jnp.maximum(m_lo, t2 + lo_bias)
                n_hi = jnp.maximum(m_hi, jnp.maximum(t1, t2 + hi_bias))
                e1 = jnp.exp2(s1 - n_hi).astype(BF16)
                e2 = jnp.exp2(s2 - jnp.where(c, n_lo, n_hi)).astype(BF16)
                m_ref[0, h] = jnp.broadcast_to(n_lo, (8, HALF))
                m_ref[1, h] = jnp.broadcast_to(n_hi, (8, HALF))
                return e1, e2, jnp.exp2(m_lo - n_lo), jnp.exp2(m_hi - n_hi)

            def gather(h, e1, e2, f_lo, f_hi):
                o_hi = jnp.dot(vt1[...], jnp.concatenate([e1, e2], axis=0), preferred_element_type=F32)
                o_lo = jnp.dot(vt2[...], e2, preferred_element_type=F32)
                acc[0, h] = acc[0, h] * f_lo + o_lo
                acc[1, h] = acc[1, h] * f_hi + o_hi

            ahead, ready = product(0), None
            for h in range(QH):
                now = ahead
                if h + 1 < QH:
                    ahead = product(h + 1)
                if ready is not None:
                    gather(h - 1, *ready)
                ready = soften(h, *now)
            gather(QH - 1, *ready)

        return carry

    lax.fori_loop(1 - AHEAD, BLOCKS, step, 0)

    for h in range(QH):
        cols = slice(h * HD, (h + 1) * HD)
        parts = []
        for s in range(2):
            total = acc[s, h, HD : HD + 1, :]
            parts.append((acc[s, h, :HD, :] / total).T)
        out[:HALF, cols] = jnp.where(swap, parts[1], parts[0]).astype(BF16)
        out[HALF:, cols] = jnp.where(swap, parts[0], parts[1]).astype(BF16)

    def drain(slot, carry):
        for piece in range(2):
            copy(0, slot, piece, peers["z"]).wait_send()
        return carry

    lax.fori_loop(1, BLOCKS, drain, 0)


def attend(pos, q, kv):
    anywhere = pl.BlockSpec(memory_space=pl.ANY)
    vmem = pl.BlockSpec(memory_space=pltpu.VMEM)
    dma = pltpu.SemaphoreType.DMA
    return pl.pallas_call(
        attend_kernel,
        out_shape=jax.ShapeDtypeStruct((TOK, QH * HD), BF16),
        in_specs=[pl.BlockSpec(memory_space=pltpu.SMEM), anywhere, anywhere],
        out_specs=vmem,
        scratch_shapes=[
            pltpu.VMEM((BLOCKS, 2, PIECE, HD), BF16),
            pltpu.VMEM((2, 2 * QH, 2 * HD, 128), BF16),
            pltpu.VMEM((HALF, HD), BF16),
            pltpu.VMEM((HD + META, 2 * HALF), BF16),
            pltpu.VMEM((HD + META, HALF), BF16),
            pltpu.VMEM((2, QH, 8, HALF), F32),
            pltpu.VMEM((2, QH, HD + META, HALF), F32),
            dma((2,)), dma((BLOCKS, 2)), dma((BLOCKS, 2)),
        ],
        compiler_params=pltpu.CompilerParams(
            collective_id=1, has_side_effects=True, vmem_limit_bytes=60 << 20),
        name="attend",
    )(pos, q, kv)


def on_device(tokens, codes, scales, down_adapter_matrix, up_adapter_matrix, positions):
    down = down_adapter_matrix.reshape(4, 2, HALF, RANK).transpose(0, 2, 1, 3).reshape(ROWS // 2, HD)
    q, kv = project(positions, tokens[0], codes, scales, down, up_adapter_matrix)
    return attend(positions, q, kv)[None]


def solution(mesh):
    return jax.shard_map(
        on_device,
        mesh=mesh,
        in_specs=(
            P("fsdp", "ctx", None), P("fsdp", None), P("fsdp", None), P("fsdp", None), P(), P("fsdp", "ctx"),
        ),
        out_specs=P("fsdp", "ctx", None),
        check_vma=False,
    )
```

```python
import jax
import jax.numpy as jnp
from jax import lax
from jax.experimental import pallas as pl
from jax.experimental.pallas import tpu as pltpu
from jax.sharding import PartitionSpec as P

MESH = pl.DeviceIdType.MESH
QH = 8
HD = 128
HEADS = QH + 2
HALF = 256
TOK = 512
WIDTH = 8192
OUT = 1280
ROWS = 2048
CHUNK = 64
RANK = 64
META = 16
PIECE = 512 + META
ROPE_BASE = 500000.0
LEVELS = (
    -1.0, -0.6961928009986877, -0.5250730514526367, -0.39491748809814453,
    -0.28444138169288635, -0.18477343022823334, -0.09105003625154495, 0.0,
    0.07958029955625534, 0.16093020141124725, 0.24611230194568634, 0.33791524171829224,
    0.44070982933044434, 0.5626170039176941, 0.7229568362236023, 1.0,
)
F32 = jnp.float32
BF16 = jnp.bfloat16
NT = (((1,), (1,)), ((), ()))
NEG = -1e30
LOG2E = 1.4426950408889634


def iota(shape, dim):
    return lax.broadcasted_iota(jnp.int32, shape, dim)


def head_order():
    p = iota((HD, HD), 1)
    return jnp.where(iota((HD, HD), 0) == 4 * (p % 32) + p // 32, 1.0, 0.0).astype(BF16)


def plane(t):
    depth = 512 if t < 8 else 256
    lane = iota((depth, HD), 1)
    column = 4 * lane + t % 4 if t < 8 else 4 * (lane % 64) + 2 * (t - 8) + lane // 64
    return (t // 4) * 512, jnp.where(iota((depth, HD), 0) == column, 1.0, 0.0).astype(BF16)


def lookup(tables, words, move):
    numbers = lax.GatherDimensionNumbers(
        offset_dims=(), collapsed_slice_dims=(0,), start_index_map=(0,),
        operand_batching_dims=(1,), start_indices_batching_dims=(1,))
    index = (words >> move) & 7
    low, high = (
        lax.gather(t, index[..., None], numbers, slice_sizes=(1, 1), mode=lax.GatherScatterMode.PROMISE_IN_BOUNDS)
        for t in tables)
    return jnp.where((words & (8 << move)) != 0, high, low)


def place():
    f, c = lax.axis_index("fsdp"), lax.axis_index("ctx")
    return f // 2, f % 2, c // 16, (c // 4) % 4, c % 4


def device(z_hi, core, z_lo, x, y):
    return (z_hi * 2 + core, z_lo * 16 + (x % 4) * 4 + y % 4)


def project_kernel(
    pos, tok_hbm, codes, scales, d_hbm, up_in, q_out, kv_out,
    wbuf, dbuf, tok, acc, accd, cos_ref, sin_ref, raw, nat, sc, up,
    local, fetched, wsend, wrecv, dsend, drecv,
):
    z_hi, core, z_lo, x, y = place()
    z = z_hi * 2 + z_lo
    cross_z = jnp.where(z % 2 == 0, (z + 3) % 4, (z + 1) % 4)
    cross = device(cross_z // 2, core, cross_z % 2, x, y)
    partner = device(z_hi, 1 - core, z_lo, x, y)
    xp, xm = device(z_hi, core, z_lo, x + 1, y), device(z_hi, core, z_lo, x + 3, y)
    yp, ym = device(z_hi, core, z_lo, x, y + 1), device(z_hi, core, z_lo, x, y + 3)
    col = (x + 2 * y) % 4

    def block(n):
        return (col * 8 + n) % 32

    def fetch(n):
        rows = pl.ds(pl.multiple_of((col + n) % 4 * 1280, 1280), 1280)
        return pltpu.make_async_copy(codes.at[rows, :], raw.at[rows, :], fetched.at[n])

    for n in range(4):
        fetch(n).start()
    tok_copy = pltpu.make_async_copy(tok_hbm, tok, local.at[0])
    own_d = pltpu.make_async_copy(d_hbm, dbuf.at[0], local.at[1])
    own_d.start()
    tok_copy.start()

    barrier = pltpu.get_barrier_semaphore()
    for peer in (cross, partner, xp, xm, yp, ym):
        pl.semaphore_signal(barrier, inc=1, device_id=peer, device_id_type=MESH)

    for t in range(HEADS):
        first, picks = plane(t)
        cols = slice(first, first + picks.shape[0])
        sc[t] = jnp.dot(scales[:, cols], picks, preferred_element_type=F32)
        half_up = 0.5 * jnp.dot(up_in[:, cols], picks, preferred_element_type=F32)
        up[:, t * HD : (t + 1) * HD] = half_up.astype(BF16)
    pl.semaphore_wait(barrier, 6)

    shift = (0, 3, 1, 2)

    def rows_of(k, c):
        quarter = (col + shift[k]) % 4
        return pl.ds(pl.multiple_of(quarter * 512 + c * CHUNK, CHUNK), CHUNK)

    def drows_of(k):
        quarter = (col + shift[k]) % 4
        return pl.ds(pl.multiple_of(quarter * 256, 256), 256)

    def wcopy(kind, c, src, dst, peer):
        return pltpu.make_async_remote_copy(
            src_ref=src, dst_ref=dst, send_sem=wsend.at[kind, c], recv_sem=wrecv.at[kind, c],
            device_id=peer, device_id_type=MESH,
        )

    def dcopy(kind, src, dst, peer):
        return pltpu.make_async_remote_copy(
            src_ref=src, dst_ref=dst, send_sem=dsend.at[kind], recv_sem=drecv.at[kind],
            device_id=peer, device_id_type=MESH,
        )

    def w_of(kind, c):
        if kind == 0:
            rows = rows_of(0, c)
            return wcopy(0, c, wbuf.at[0, rows, :], wbuf.at[2, rows, :], cross)
        if kind in (1, 2, 3):
            rows = rows_of(0, c)
            peer = xp if kind == 1 else xm if kind == 2 else (yp, ym)[c % 2]
            return wcopy(kind, c, wbuf.at[2, rows, :], wbuf.at[2, rows, :], peer)
        if kind == 4:
            rows = pl.ds(pl.multiple_of((col + c) % 4 * 512, 512), 512)
            return wcopy(4, c, wbuf.at[0, rows, :], wbuf.at[1, rows, :], partner)
        rows = rows_of(kind - 5, c)
        return wcopy(kind, c, wbuf.at[2, rows, :], wbuf.at[3, rows, :], partner)

    def d_of(kind):
        if kind == 0:
            rows = drows_of(0)
            return dcopy(0, d_hbm.at[rows, :], dbuf.at[2, rows, :], cross)
        if kind in (1, 2, 3):
            rows = drows_of(0)
            return dcopy(kind, dbuf.at[2, rows, :], dbuf.at[2, rows, :], (xp, xm, yp)[kind - 1])
        if kind == 4:
            return dcopy(4, d_hbm, dbuf.at[1], partner)
        rows = drows_of(kind - 5)
        return dcopy(kind, dbuf.at[2, rows, :], dbuf.at[3, rows, :], partner)

    d_of(0).start()
    d_of(4).start()

    left = iota((8, HD), 1) < 64
    place_in = iota((64, HD), 1)
    digit = 4 * (place_in // 64)
    tables = []
    for first in (0, 8):
        table = jnp.zeros((8, HD), F32)
        for n in range(8):
            table = jnp.where(iota((8, HD), 0) == n, LEVELS[first + n], table)
        tables.append(table)

    def dequantize(n, slot):
        b = block(n)
        for g in range(4):
            u = [raw[pl.ds(b // 8 * 1280 + 8 * (40 * g + i) + b % 8, 8, stride=40), :] for i in range(5)]
            r2, r3, r4 = (pltpu.roll(u[i], 64, 1) for i in (2, 3, 4))
            odd = (jnp.where(left, r2, r3), jnp.where(left, r3, r4), r4)
            for j in range(3):
                nat[slot, j, pl.ds(16 * g, 8, stride=2), :] = u[j]
                nat[slot, j, pl.ds(16 * g + 1, 8, stride=2), :] = odd[j]

    def levels(n, slot):
        b = block(n)
        rows = pl.ds(pl.multiple_of(b * 64, 64), 64)
        for t in range(HEADS):
            words = nat[slot, t // 4]
            if t < 8:
                move = 4 * (t % 4)
            else:
                words = jnp.where(place_in < 64, words, pltpu.roll(words, 64, 1))
                move = digit + 8 * (t - 8)
            level = jnp.concatenate(
                [lookup(tables, words[r : r + 8], move if t < 8 else move[:8]) for r in range(0, 64, 8)], axis=0)
            wbuf[0, rows, t * HD : (t + 1) * HD] = (level * sc[t, pl.ds(b, 1), :]).astype(BF16)

    def arrive(c):
        w_of(0, c).wait_recv()
        for kind in (1, 2, 3, 5):
            w_of(kind, c).start()
        if c == 0:
            d_of(0).wait_recv()
            for kind in (1, 2, 3, 5):
                d_of(kind).start()

    def onward(c):
        for kind in (1, 2, 3):
            w_of(kind, c).wait_recv()
            w_of(5 + kind, c).start()
        if c == 0:
            for kind in (1, 2, 3):
                d_of(kind).wait_recv()
                d_of(5 + kind).start()

    def from_partner(kinds, cs):
        for kind in kinds:
            for c in cs:
                w_of(5 + kind, c).wait_recv()
            if 0 in cs:
                d_of(5 + kind).wait_recv()

    def pair(n, carry):
        for k in range(4):
            @pl.when(n == 4 * k)
            def _():
                fetch(k).wait()

        dequantize(2 * n, 0)
        dequantize(2 * n + 1, 1)
        levels(2 * n, 0)
        levels(2 * n + 1, 1)

        @pl.when(n <= 4)
        def _():
            for c in range(4):
                @pl.when(n == c + 1)
                def _():
                    w_of(0, 2 * c).start()
                    w_of(0, 2 * c + 1).start()

        @pl.when(n == 10)
        def _():
            arrive(0)

        @pl.when((n > 0) & (n % 4 == 0))
        def _():
            for c in range(3):
                @pl.when(n == 4 * c + 4)
                def _():
                    w_of(4, c).start()

        return carry

    lax.fori_loop(0, 16, pair, 0)

    row = iota((64, TOK), 0)
    lane = iota((64, TOK), 1)
    index = (4 * (row % 16) + row // 16).astype(F32)
    inverse = jnp.exp(-jnp.log(F32(ROPE_BASE)) * 2.0 * index / HD)
    token_pos = jnp.where(lane < HALF, lane + pos[0, 0], lane - HALF + pos[0, HALF])
    angle = token_pos.astype(F32) * inverse
    cos_ref[...] = jnp.cos(angle)
    sin_ref[...] = jnp.sin(angle)

    w_of(4, 3).start()
    acc[...] = jnp.zeros_like(acc)
    accd[...] = jnp.zeros_like(accd)
    tok_copy.wait()
    own_d.wait()

    def early(u, carry):
        @pl.when(u == 0)
        def _():
            arrive(1)

        @pl.when(u == 2)
        def _():
            onward(0)
            arrive(2)

        @pl.when(u == 4)
        def _():
            onward(1)
            arrive(3)
            d_of(4).wait_recv()

        @pl.when(u == 7)
        def _():
            onward(2)
            arrive(4)

        for k in range(4):
            @pl.when(u == 4 + k)
            def _():
                w_of(4, k).wait_recv()

        slot = u // 4
        quarter = (col + u % 4) % 4
        base = quarter * 512
        owner = z_hi * 2 + jnp.where(slot == 0, core, 1 - core)
        t = tok[:, pl.ds(pl.multiple_of(owner * ROWS + base, 512), 512)]
        acc[...] += jnp.dot(
            t, wbuf[slot, pl.ds(pl.multiple_of(base, 512), 512), :], preferred_element_type=F32)
        d = dbuf[slot, pl.ds(pl.multiple_of(quarter * 256, 256), 256), :]
        for part in range(2):
            accd[part] += jnp.dot(t[:, part * 256 : part * 256 + 256], d, preferred_element_type=F32)
        return carry

    lax.fori_loop(0, 8, early, 0)

    def source(slot, kind):
        moved = jnp.where(kind == 1, 3, jnp.where(kind == 2, 1, jnp.where(kind == 3, 2, 0)))
        return (col + moved) % 4, (1 - z_hi) * 2 + jnp.where(slot == 2, core, 1 - core)

    def late(u, carry):
        @pl.when(u == 1)
        def _():
            from_partner((0,), (0, 1, 2, 3))

        @pl.when(u == 2)
        def _():
            onward(3)
            arrive(5)

        @pl.when(u == 5)
        def _():
            from_partner((1, 2, 3), (0, 1, 2, 3))

        @pl.when(u == 6)
        def _():
            onward(4)
            arrive(6)

        @pl.when(u == 8)
        def _():
            onward(5)
            arrive(7)

        @pl.when(u == 9)
        def _():
            from_partner((0,), (4, 5, 6, 7))

        part = u // 8
        v = u % 8
        slot = jnp.where(v < 2, 2 + v, 2 + (v - 2) // 3)
        kind = jnp.where(v < 2, 0, 1 + (v - 2) % 3)
        quarter, owner = source(slot, kind)
        base = quarter * 512 + part * 256
        t = tok[:, pl.ds(pl.multiple_of(owner * ROWS + base, 256), 256)]
        acc[...] += jnp.dot(
            t, wbuf[slot, pl.ds(pl.multiple_of(base, 256), 256), :], preferred_element_type=F32)
        accd[part] += jnp.dot(
            t, dbuf[slot, pl.ds(pl.multiple_of(quarter * 256, 256), 256), :], preferred_element_type=F32)
        return carry

    lax.fori_loop(0, 10, late, 0)

    def last(u, carry):
        @pl.when(u == 1)
        def _():
            from_partner((1, 2, 3), (4, 5))
            onward(6)

        @pl.when(u == 3)
        def _():
            onward(7)

        @pl.when(u == 4)
        def _():
            from_partner((1, 2, 3), (6, 7))

        part = u // 3
        ts, ws, ds = [], [], []
        for n in range(2):
            i = 2 * (u % 3) + n
            slot = 2 + i // 3
            quarter, owner = source(slot, 1 + i % 3)
            base = quarter * 512 + 256 + part * 128
            ts.append(tok[:, pl.ds(pl.multiple_of(owner * ROWS + base, 128), 128)])
            ws.append(wbuf[slot, pl.ds(pl.multiple_of(base, 128), 128), :])
            ds.append(dbuf[slot, pl.ds(pl.multiple_of(quarter * 256 + part * 128, 128), 128), :])
        t = jnp.concatenate(ts, axis=1)
        acc[...] += jnp.dot(t, jnp.concatenate(ws, axis=0), preferred_element_type=F32)
        accd[1] += jnp.dot(t, jnp.concatenate(ds, axis=0), preferred_element_type=F32)
        return carry

    lax.fori_loop(0, 6, last, 0)

    low = (accd[0] + pltpu.roll(accd[1], 64, 1)).astype(BF16)[:, :RANK]
    start0, start1 = pos[0, 0], pos[0, HALF]
    swap = start0 > start1
    lower = jnp.where(swap, start1, start0)
    pair = jnp.where(iota((HD, 2 * HD), 0) == iota((HD, 2 * HD), 1) % HD, 1.0, 0.0).astype(BF16)

    def joined(t):
        cols = slice(t * HD, (t + 1) * HD)
        full = acc[:, cols] + jnp.dot(low, up[:, cols], preferred_element_type=F32)
        high = full.astype(BF16)
        rest = (full - high.astype(F32)).astype(BF16)
        return lax.dot_general(pair, jnp.concatenate([high, rest], axis=1), NT, preferred_element_type=F32)

    def rope(u, k):
        c, n = cos_ref[16 * k : 16 * k + 16, :], sin_ref[16 * k : 16 * k + 16, :]
        return jnp.concatenate([u[:16] * c - u[16:] * n, u[16:] * c + u[:16] * n], axis=0)

    def halves(a, axis):
        lo = lax.slice_in_dim(a, 0, HALF, axis=axis)
        hi = lax.slice_in_dim(a, HALF, TOK, axis=axis)
        return jnp.where(swap, hi, lo), jnp.where(swap, lo, hi)

    ahead = joined(0)
    for j in range(2):
        for k in range(4):
            turned = ahead
            ahead = joined(4 * j + k + 1)
            for t in range(4):
                q = (rope(turned[32 * t : 32 * t + 32], k) * HD ** (-0.5)).astype(BF16).astype(F32) * LOG2E
                for s, part in enumerate(halves(q, 1)):
                    high = part.astype(BF16)
                    rest = (part - high.astype(F32)).astype(BF16)
                    for n in range(2):
                        tile = 2 * (4 * j + t) + n
                        q_out[s, tile, 32 * k : 32 * k + 32, :] = high[:, n * 128 : n * 128 + 128]
                        q_out[s, tile, HD + 32 * k : HD + 32 * k + 32, :] = rest[:, n * 128 : n * 128 + 128]
    both = (ahead, joined(9))
    key = jnp.concatenate(
        [rope(both[k // 2][64 * (k % 2) : 64 * (k % 2) + 32], k) for k in range(4)], axis=0)
    for s, part in enumerate(halves(key.T, 0)):
        kv_out[s, :HALF, :] = part.astype(BF16)
    value = jnp.concatenate(
        [both[k // 2][64 * (k % 2) + 32 : 64 * (k % 2) + 64] for k in range(4)], axis=0).astype(BF16)
    vt = jnp.dot(head_order(), value, preferred_element_type=F32)
    for s, part in enumerate(halves(vt, 1)):
        kv_out[s, HALF : HALF + 128, :] = part[:, :128].astype(BF16)
        kv_out[s, HALF + 128 : HALF + 256, :] = part[:, 128:].astype(BF16)
        kv_out[s, 2 * HALF :, :] = (jnp.zeros((META, HD), F32) + (lower // HALF).astype(F32)).astype(BF16)

    for kind in range(9):
        for c in range(4 if kind == 4 else 8):
            w_of(kind, c).wait_send()
    for kind in range(9):
        d_of(kind).wait_send()


def project(pos, tokens, codes, scales, down, up):
    view = codes.reshape(4, 8, 160, HD).transpose(0, 2, 1, 3).reshape(5120, HD)
    anywhere = pl.BlockSpec(memory_space=pl.ANY)
    vmem = pl.BlockSpec(memory_space=pltpu.VMEM)
    dma = pltpu.SemaphoreType.DMA
    return pl.pallas_call(
        project_kernel,
        out_shape=(
            jax.ShapeDtypeStruct((2, 2 * QH, 2 * HD, 128), BF16),
            jax.ShapeDtypeStruct((2, PIECE, HD), BF16),
        ),
        in_specs=[pl.BlockSpec(memory_space=pltpu.SMEM), anywhere, anywhere, vmem, anywhere, vmem],
        out_specs=(vmem, vmem),
        scratch_shapes=[
            pltpu.VMEM((4, ROWS, OUT), BF16),
            pltpu.VMEM((4, ROWS // 2, HD), BF16),
            pltpu.VMEM((TOK, WIDTH), BF16),
            pltpu.VMEM((TOK, OUT), F32),
            pltpu.VMEM((2, TOK, HD), F32),
            pltpu.VMEM((64, TOK), F32),
            pltpu.VMEM((64, TOK), F32),
            pltpu.VMEM((5120, HD), jnp.int32),
            pltpu.VMEM((2, 3, 64, HD), jnp.int32),
            pltpu.VMEM((HEADS, 32, HD), F32),
            pltpu.VMEM((RANK, OUT), BF16),
            dma((2,)), dma((4,)), dma((9, 8)), dma((9, 8)), dma((9,)), dma((9,)),
        ],
        compiler_params=pltpu.CompilerParams(
            collective_id=0, has_side_effects=True, vmem_limit_bytes=60 << 20),
        name="project",
    )(pos, tokens, view, scales, down, up)


ORDER = (
    (0, 0, 0), (0, 1, 0), (0, 3, 0), (0, 0, 1), (0, 0, 3), (1, 0, 0), (0, 2, 0), (0, 0, 2),
    (0, 1, 3), (0, 1, 1), (0, 3, 3), (1, 1, 0), (0, 3, 1), (1, 3, 0), (0, 2, 1), (1, 0, 1),
    (0, 2, 3), (0, 1, 2), (1, 0, 3), (1, 3, 1), (1, 1, 1), (0, 3, 2), (1, 3, 3), (1, 1, 3),
    (1, 2, 0), (1, 2, 1), (0, 2, 2), (1, 0, 2), (1, 2, 3), (1, 3, 2), (1, 1, 2), (1, 2, 2),
)
SLOT = {s: i for i, s in enumerate(ORDER)}
BLOCKS = len(ORDER)
PAIRS = BLOCKS // 2


def routes():
    table = {}
    for p in (0, 1):
        table[(0, 1, 0), p] = ("xp", (0, 0, 0))
        table[(0, 3, 0), p] = ("xm", (0, 0, 0))
        for dx in range(4):
            table[(0, dx, 1), p] = ("yp", (0, dx, 0))
            table[(0, dx, 3), p] = ("ym", (0, dx, 0))
        for s in ((0, 0), (1, 0), (3, 0), (2, 0), (0, 1), (0, 3)):
            table[(1,) + s, p] = ("z", (0,) + s)
        for dy in (1, 2, 3):
            table[(1, 1, dy), p] = ("xp", (1, 0, dy))
            table[(1, 3, dy), p] = ("xm", (1, 0, dy))
    table[(0, 2, 0), 0] = ("xm", (0, 3, 0))
    table[(0, 2, 0), 1] = ("xp", (0, 1, 0))
    for dx in range(4):
        table[(0, dx, 2), 0] = ("ym", (0, dx, 3))
        table[(0, dx, 2), 1] = ("yp", (0, dx, 1))
    table[(1, 0, 2), 0] = ("ym", (1, 0, 3))
    table[(1, 0, 2), 1] = ("yp", (1, 0, 1))
    for dy in (1, 2, 3):
        table[(1, 2, dy), 0] = ("xm", (1, 3, dy))
        table[(1, 2, dy), 1] = ("xp", (1, 1, dy))
    return table


def forwards():
    opposite = {"xp": "xm", "xm": "xp", "yp": "ym", "ym": "yp", "z": "z"}
    table = {i: [] for i in range(BLOCKS)}
    for (s, p), (origin, source) in routes().items():
        table[SLOT[source]].append((SLOT[s], p, opposite[origin]))
    return {i: sorted(v) for i, v in table.items()}


def attend_kernel(pos, q_in, kv, out, kvbuf, q, k2, vt1, vt2, m_ref, acc, local, send, recv):
    z_hi, core, z_lo, x, y = place()
    peers = {
        "xp": device(z_hi, core, z_lo, x + 1, y), "xm": device(z_hi, core, z_lo, x + 3, y),
        "yp": device(z_hi, core, z_lo, x, y + 1), "ym": device(z_hi, core, z_lo, x, y + 3),
        "z": device(z_hi, core, 1 - z_lo, x, y),
    }
    table = forwards()
    own = pltpu.make_async_copy(kv, kvbuf.at[0], local.at[0])
    own_q = pltpu.make_async_copy(q_in, q, local.at[1])
    own.start()
    own_q.start()
    barrier = pltpu.get_barrier_semaphore()
    for peer in peers.values():
        pl.semaphore_signal(barrier, inc=1, device_id=peer, device_id_type=MESH)
    pl.semaphore_wait(barrier, len(peers))
    own.wait()

    def copy(source, slot, piece, peer):
        return pltpu.make_async_remote_copy(
            src_ref=kvbuf.at[source, piece], dst_ref=kvbuf.at[slot, piece],
            send_sem=send.at[slot, piece], recv_sem=recv.at[slot, piece],
            device_id=peer, device_id_type=MESH,
        )

    def forward(source):
        for slot, piece, to in table[source]:
            copy(source, slot, piece, peers[to]).start()

    def take(slot):
        for piece in range(2):
            copy(0, slot, piece, peers["z"]).wait_recv()

    forward(0)

    start0, start1 = pos[0, 0], pos[0, HALF]
    swap = start0 > start1
    mine = (jnp.where(swap, start1, start0) // HALF).astype(F32)
    one = jnp.ones((META, HALF), BF16)
    for n in range(2):
        vt1[n, HD:, :HALF] = one
        vt2[n, HD:, :] = one

    def query(s, h):
        return jnp.concatenate([q[s, 2 * h], q[s, 2 * h + 1]], axis=1)

    def keys(slot, piece):
        return kvbuf[slot, piece, :HALF, :]

    def values(slot, piece):
        return jnp.concatenate(
            [kvbuf[slot, piece, HALF : HALF + 128, :], kvbuf[slot, piece, HALF + 128 : HALF + 256, :]], axis=1)

    def scores(k, qt):
        return jnp.dot(jnp.concatenate([k, k], axis=1), qt, preferred_element_type=F32)

    def top(s):
        return jnp.max(s, axis=0, keepdims=True)

    own_q.wait()
    def pipeline(units, product, soften, gather):
        ahead, ready = product(*units[0]), None
        for n, unit in enumerate(units):
            now = ahead
            if n + 1 < len(units):
                ahead = product(*units[n + 1])
            if ready is not None:
                gather(*units[n - 1], *ready)
            ready = soften(*unit, *now)
        gather(*units[-1], *ready)

    vt1[0, :HD, :HALF] = values(0, 0)
    vt2[0, :HD, :] = values(0, 1)
    k2[0] = keys(0, 1)
    seen = iota((HALF, HALF), 0) <= iota((HALF, HALF), 1)

    def own_product(h):
        q0, q1 = query(0, h), query(1, h)
        return scores(keys(0, 0), q0), scores(keys(0, 0), q1), scores(k2[0], q1)

    def own_soften(h, s00, s10, s11):
        s00, s11 = jnp.where(seen, s00, -jnp.inf), jnp.where(seen, s11, -jnp.inf)
        m0, m1 = top(s00), jnp.maximum(top(s10), top(s11))
        m_ref[0, h] = jnp.broadcast_to(m0, (8, HALF))
        m_ref[1, h] = jnp.broadcast_to(m1, (8, HALF))
        return [jnp.exp2(x - m).astype(BF16) for x, m in ((s00, m0), (s10, m1), (s11, m1))]

    def own_gather(h, e00, e10, e11):
        def weigh(vt, e):
            return jnp.dot(vt, e, preferred_element_type=F32)

        acc[0, h] = weigh(vt1[0, :, :HALF], e00)
        acc[1, h] = weigh(vt1[0, :, :HALF], e10) + weigh(vt2[0], e11)

    pipeline([(h,) for h in range(QH)], own_product, own_soften, own_gather)

    def blocks(slots):
        low, lo_bias, hi_bias = [], [], []
        zero = jnp.zeros((HD, HALF), BF16)
        for n, i in enumerate(slots):
            c = jnp.max(kvbuf[i, 0, 2 * HALF :, :].astype(F32)) < mine
            low.append(c)
            lo_bias.append(jnp.where(c, 0.0, NEG))
            hi_bias.append(jnp.where(c, NEG, 0.0))
            low_v = values(i, 0)
            k2[n] = jnp.where(c, keys(i, 0), keys(i, 1))
            vt1[n, :HD, :HALF] = low_v
            vt1[n, :HD, HALF:] = jnp.where(c, zero, values(i, 1))
            vt1[n, HD:, HALF:] = jnp.where(c, zero[:META], one)
            vt2[n, :HD, :] = jnp.where(c, low_v, zero)
            vt2[n, HD:, :] = jnp.where(c, one, zero[:META])

        def product(n, h):
            q1 = query(1, h)
            q2 = jnp.where(low[n], query(0, h), q1)
            return scores(keys(slots[n], 0), q1), scores(k2[n], q2)

        def soften(n, h, s1, s2):
            t1, t2 = top(s1), top(s2)
            m_lo, m_hi = m_ref[0, h, :1, :], m_ref[1, h, :1, :]
            n_lo = jnp.maximum(m_lo, t2 + lo_bias[n])
            n_hi = jnp.maximum(m_hi, jnp.maximum(t1, t2 + hi_bias[n]))
            e1 = jnp.exp2(s1 - n_hi).astype(BF16)
            e2 = jnp.exp2(s2 - jnp.where(low[n], n_lo, n_hi)).astype(BF16)
            m_ref[0, h] = jnp.broadcast_to(n_lo, (8, HALF))
            m_ref[1, h] = jnp.broadcast_to(n_hi, (8, HALF))
            return e1, e2, jnp.exp2(m_lo - n_lo), jnp.exp2(m_hi - n_hi)

        def gather(n, h, e1, e2, f_lo, f_hi):
            o_hi = jnp.dot(vt1[n], jnp.concatenate([e1, e2], axis=0), preferred_element_type=F32)
            o_lo = jnp.dot(vt2[n], e2, preferred_element_type=F32)
            acc[0, h] = acc[0, h] * f_lo + o_lo
            acc[1, h] = acc[1, h] * f_hi + o_hi

        pipeline([(n, h) for n in range(len(slots)) for h in range(QH)], product, soften, gather)

    def step(p, carry):
        def come(k):
            @pl.when(p + 1 == k)
            def _():
                for slot in (2 * k - 1, 2 * k):
                    if slot < BLOCKS:
                        take(slot)
                        forward(slot)

        for group in range(0, PAIRS + 1, 4):
            @pl.when((p + 1 >= group) & (p + 1 < group + 4))
            def _():
                for k in range(max(group, 1), min(group + 4, PAIRS + 1)):
                    come(k)

        @pl.when(p > 0)
        def _():
            blocks((2 * p - 1, 2 * p))

        return carry

    lax.fori_loop(0, PAIRS, step, 0)
    blocks((BLOCKS - 1,))

    for h in range(QH):
        cols = slice(h * HD, (h + 1) * HD)
        parts = []
        for s in range(2):
            total = acc[s, h, HD : HD + 1, :]
            parts.append((acc[s, h, :HD, :] / total).T)
        out[:HALF, cols] = jnp.where(swap, parts[1], parts[0]).astype(BF16)
        out[HALF:, cols] = jnp.where(swap, parts[0], parts[1]).astype(BF16)

    def drain(slot, carry):
        for piece in range(2):
            copy(0, slot, piece, peers["z"]).wait_send()
        return carry

    lax.fori_loop(1, BLOCKS, drain, 0)


def attend(pos, q, kv):
    anywhere = pl.BlockSpec(memory_space=pl.ANY)
    vmem = pl.BlockSpec(memory_space=pltpu.VMEM)
    dma = pltpu.SemaphoreType.DMA
    return pl.pallas_call(
        attend_kernel,
        out_shape=jax.ShapeDtypeStruct((TOK, QH * HD), BF16),
        in_specs=[pl.BlockSpec(memory_space=pltpu.SMEM), anywhere, anywhere],
        out_specs=vmem,
        scratch_shapes=[
            pltpu.VMEM((BLOCKS, 2, PIECE, HD), BF16),
            pltpu.VMEM((2, 2 * QH, 2 * HD, 128), BF16),
            pltpu.VMEM((2, HALF, HD), BF16),
            pltpu.VMEM((2, HD + META, 2 * HALF), BF16),
            pltpu.VMEM((2, HD + META, HALF), BF16),
            pltpu.VMEM((2, QH, 8, HALF), F32),
            pltpu.VMEM((2, QH, HD + META, HALF), F32),
            dma((2,)), dma((BLOCKS, 2)), dma((BLOCKS, 2)),
        ],
        compiler_params=pltpu.CompilerParams(
            collective_id=1, has_side_effects=True, vmem_limit_bytes=60 << 20),
        name="attend",
    )(pos, q, kv)


def on_device(tokens, codes, scales, down_adapter_matrix, up_adapter_matrix, positions):
    down = down_adapter_matrix.reshape(4, 2, HALF, RANK).transpose(0, 2, 1, 3).reshape(ROWS // 2, HD)
    q, kv = project(positions, tokens[0], codes, scales, down, up_adapter_matrix)
    return attend(positions, q, kv)[None]


def solution(mesh):
    return jax.shard_map(
        on_device,
        mesh=mesh,
        in_specs=(
            P("fsdp", "ctx", None), P("fsdp", None), P("fsdp", None), P("fsdp", None), P(), P("fsdp", "ctx"),
        ),
        out_specs=P("fsdp", "ctx", None),
        check_vma=False,
    )
```

```python
import jax
import jax.numpy as jnp
from jax import lax
from jax.experimental import pallas as pl
from jax.experimental.pallas import tpu as pltpu
from jax.sharding import PartitionSpec as P

MESH = pl.DeviceIdType.MESH
QH = 8
HD = 128
HEADS = QH + 2
HALF = 256
TOK = 512
WIDTH = 8192
OUT = 1280
ROWS = 2048
CHUNK = 64
RANK = 64
META = 16
PIECE = 512 + META
ROPE_BASE = 500000.0
LEVELS = (
    -1.0, -0.6961928009986877, -0.5250730514526367, -0.39491748809814453,
    -0.28444138169288635, -0.18477343022823334, -0.09105003625154495, 0.0,
    0.07958029955625534, 0.16093020141124725, 0.24611230194568634, 0.33791524171829224,
    0.44070982933044434, 0.5626170039176941, 0.7229568362236023, 1.0,
)
F32 = jnp.float32
BF16 = jnp.bfloat16
NT = (((1,), (1,)), ((), ()))
NEG = -1e30
LOG2E = 1.4426950408889634


def iota(shape, dim):
    return lax.broadcasted_iota(jnp.int32, shape, dim)


def head_order():
    p = iota((HD, HD), 1)
    return jnp.where(iota((HD, HD), 0) == 4 * (p % 32) + p // 32, 1.0, 0.0).astype(BF16)


def plane(t):
    depth = 512 if t < 8 else 256
    lane = iota((depth, HD), 1)
    column = 4 * lane + t % 4 if t < 8 else 4 * (lane % 64) + 2 * (t - 8) + lane // 64
    return (t // 4) * 512, jnp.where(iota((depth, HD), 0) == column, 1.0, 0.0).astype(BF16)


def lookup(tables, words, move):
    numbers = lax.GatherDimensionNumbers(
        offset_dims=(), collapsed_slice_dims=(0,), start_index_map=(0,),
        operand_batching_dims=(1,), start_indices_batching_dims=(1,))
    index = (words >> move) & 7
    low, high = (
        lax.gather(t, index[..., None], numbers, slice_sizes=(1, 1), mode=lax.GatherScatterMode.PROMISE_IN_BOUNDS)
        for t in tables)
    return jnp.where((words & (8 << move)) != 0, high, low)


def place():
    f, c = lax.axis_index("fsdp"), lax.axis_index("ctx")
    return f // 2, f % 2, c // 16, (c // 4) % 4, c % 4


def device(z_hi, core, z_lo, x, y):
    return (z_hi * 2 + core, z_lo * 16 + (x % 4) * 4 + y % 4)


def project_kernel(
    pos, tok_hbm, codes, scales, d_hbm, up_in, q_out, kv_out,
    wbuf, dbuf, tok, acc, accd, cos_ref, sin_ref, raw, nat, sc, up,
    local, fetched, wsend, wrecv, dsend, drecv,
):
    z_hi, core, z_lo, x, y = place()
    z = z_hi * 2 + z_lo
    cross_z = jnp.where(z % 2 == 0, (z + 3) % 4, (z + 1) % 4)
    cross = device(cross_z // 2, core, cross_z % 2, x, y)
    partner = device(z_hi, 1 - core, z_lo, x, y)
    xp, xm = device(z_hi, core, z_lo, x + 1, y), device(z_hi, core, z_lo, x + 3, y)
    yp, ym = device(z_hi, core, z_lo, x, y + 1), device(z_hi, core, z_lo, x, y + 3)
    col = (x + 2 * y) % 4

    def block(n):
        return (col * 8 + n) % 32

    def fetch(n):
        rows = pl.ds(pl.multiple_of((col + n) % 4 * 1280, 1280), 1280)
        return pltpu.make_async_copy(codes.at[rows, :], raw.at[rows, :], fetched.at[n])

    for n in range(4):
        fetch(n).start()
    tok_copy = pltpu.make_async_copy(tok_hbm, tok, local.at[0])
    own_d = pltpu.make_async_copy(d_hbm, dbuf.at[0], local.at[1])
    own_d.start()
    tok_copy.start()

    barrier = pltpu.get_barrier_semaphore()
    for peer in (cross, partner, xp, xm, yp, ym):
        pl.semaphore_signal(barrier, inc=1, device_id=peer, device_id_type=MESH)

    for t in range(HEADS):
        first, picks = plane(t)
        cols = slice(first, first + picks.shape[0])
        sc[t] = jnp.dot(scales[:, cols], picks, preferred_element_type=F32)
        half_up = 0.5 * jnp.dot(up_in[:, cols], picks, preferred_element_type=F32)
        up[:, t * HD : (t + 1) * HD] = half_up.astype(BF16)
    pl.semaphore_wait(barrier, 6)

    shift = (0, 3, 1, 2)

    def rows_of(k, c):
        quarter = (col + shift[k]) % 4
        return pl.ds(pl.multiple_of(quarter * 512 + c * CHUNK, CHUNK), CHUNK)

    def drows_of(k):
        quarter = (col + shift[k]) % 4
        return pl.ds(pl.multiple_of(quarter * 256, 256), 256)

    def wcopy(kind, c, src, dst, peer):
        return pltpu.make_async_remote_copy(
            src_ref=src, dst_ref=dst, send_sem=wsend.at[kind, c], recv_sem=wrecv.at[kind, c],
            device_id=peer, device_id_type=MESH,
        )

    def dcopy(kind, src, dst, peer):
        return pltpu.make_async_remote_copy(
            src_ref=src, dst_ref=dst, send_sem=dsend.at[kind], recv_sem=drecv.at[kind],
            device_id=peer, device_id_type=MESH,
        )

    def w_of(kind, c):
        if kind == 0:
            rows = rows_of(0, c)
            return wcopy(0, c, wbuf.at[0, rows, :], wbuf.at[2, rows, :], cross)
        if kind in (1, 2, 3):
            rows = rows_of(0, c)
            peer = xp if kind == 1 else xm if kind == 2 else (yp, ym)[c % 2]
            return wcopy(kind, c, wbuf.at[2, rows, :], wbuf.at[2, rows, :], peer)
        if kind == 4:
            rows = pl.ds(pl.multiple_of((col + c) % 4 * 512, 512), 512)
            return wcopy(4, c, wbuf.at[0, rows, :], wbuf.at[1, rows, :], partner)
        rows = rows_of(kind - 5, c)
        return wcopy(kind, c, wbuf.at[2, rows, :], wbuf.at[3, rows, :], partner)

    def d_of(kind):
        if kind == 0:
            rows = drows_of(0)
            return dcopy(0, d_hbm.at[rows, :], dbuf.at[2, rows, :], cross)
        if kind in (1, 2, 3):
            rows = drows_of(0)
            return dcopy(kind, dbuf.at[2, rows, :], dbuf.at[2, rows, :], (xp, xm, yp)[kind - 1])
        if kind == 4:
            return dcopy(4, d_hbm, dbuf.at[1], partner)
        rows = drows_of(kind - 5)
        return dcopy(kind, dbuf.at[2, rows, :], dbuf.at[3, rows, :], partner)

    d_of(0).start()
    d_of(4).start()

    left = iota((8, HD), 1) < 64
    place_in = iota((64, HD), 1)
    digit = 4 * (place_in // 64)
    tables = []
    for first in (0, 8):
        table = jnp.zeros((8, HD), F32)
        for n in range(8):
            table = jnp.where(iota((8, HD), 0) == n, LEVELS[first + n], table)
        tables.append(table)

    def dequantize(n, slot):
        b = block(n)
        for g in range(4):
            u = [raw[pl.ds(b // 8 * 1280 + 8 * (40 * g + i) + b % 8, 8, stride=40), :] for i in range(5)]
            r2, r3, r4 = (pltpu.roll(u[i], 64, 1) for i in (2, 3, 4))
            odd = (jnp.where(left, r2, r3), jnp.where(left, r3, r4), r4)
            for j in range(3):
                nat[slot, j, pl.ds(16 * g, 8, stride=2), :] = u[j]
                nat[slot, j, pl.ds(16 * g + 1, 8, stride=2), :] = odd[j]

    def levels(n, slot):
        b = block(n)
        rows = pl.ds(pl.multiple_of(b * 64, 64), 64)
        for t in range(HEADS):
            words = nat[slot, t // 4]
            if t < 8:
                move = 4 * (t % 4)
            else:
                words = jnp.where(place_in < 64, words, pltpu.roll(words, 64, 1))
                move = digit + 8 * (t - 8)
            level = jnp.concatenate(
                [lookup(tables, words[r : r + 8], move if t < 8 else move[:8]) for r in range(0, 64, 8)], axis=0)
            wbuf[0, rows, t * HD : (t + 1) * HD] = (level * sc[t, pl.ds(b, 1), :]).astype(BF16)

    def arrive(c):
        w_of(0, c).wait_recv()
        for kind in (1, 2, 3, 5):
            w_of(kind, c).start()
        if c == 0:
            d_of(0).wait_recv()
            for kind in (1, 2, 3, 5):
                d_of(kind).start()

    def onward(c):
        for kind in (1, 2, 3):
            w_of(kind, c).wait_recv()
            w_of(5 + kind, c).start()
        if c == 0:
            for kind in (1, 2, 3):
                d_of(kind).wait_recv()
                d_of(5 + kind).start()

    def from_partner(kinds, cs):
        for kind in kinds:
            for c in cs:
                w_of(5 + kind, c).wait_recv()
            if 0 in cs:
                d_of(5 + kind).wait_recv()

    def pair(n, carry):
        for k in range(4):
            @pl.when(n == 4 * k)
            def _():
                fetch(k).wait()

        dequantize(2 * n, 0)
        dequantize(2 * n + 1, 1)
        levels(2 * n, 0)
        levels(2 * n + 1, 1)

        @pl.when(n <= 4)
        def _():
            for c in range(4):
                @pl.when(n == c + 1)
                def _():
                    w_of(0, 2 * c).start()
                    w_of(0, 2 * c + 1).start()

        @pl.when(n == 10)
        def _():
            arrive(0)

        @pl.when((n > 0) & (n % 4 == 0))
        def _():
            for c in range(3):
                @pl.when(n == 4 * c + 4)
                def _():
                    w_of(4, c).start()

        return carry

    lax.fori_loop(0, 16, pair, 0)

    row = iota((64, TOK), 0)
    lane = iota((64, TOK), 1)
    index = (4 * (row % 16) + row // 16).astype(F32)
    inverse = jnp.exp(-jnp.log(F32(ROPE_BASE)) * 2.0 * index / HD)
    token_pos = jnp.where(lane < HALF, lane + pos[0, 0], lane - HALF + pos[0, HALF])
    angle = token_pos.astype(F32) * inverse
    cos_ref[...] = jnp.cos(angle)
    sin_ref[...] = jnp.sin(angle)

    w_of(4, 3).start()
    acc[...] = jnp.zeros_like(acc)
    accd[...] = jnp.zeros_like(accd)
    tok_copy.wait()
    own_d.wait()

    def early(u, carry):
        @pl.when(u == 0)
        def _():
            arrive(1)

        @pl.when(u == 2)
        def _():
            onward(0)
            arrive(2)

        @pl.when(u == 4)
        def _():
            onward(1)
            arrive(3)
            d_of(4).wait_recv()

        @pl.when(u == 7)
        def _():
            onward(2)
            arrive(4)

        for k in range(4):
            @pl.when(u == 4 + k)
            def _():
                w_of(4, k).wait_recv()

        slot = u // 4
        quarter = (col + u % 4) % 4
        base = quarter * 512
        owner = z_hi * 2 + jnp.where(slot == 0, core, 1 - core)
        t = tok[:, pl.ds(pl.multiple_of(owner * ROWS + base, 512), 512)]
        acc[...] += jnp.dot(
            t, wbuf[slot, pl.ds(pl.multiple_of(base, 512), 512), :], preferred_element_type=F32)
        d = dbuf[slot, pl.ds(pl.multiple_of(quarter * 256, 256), 256), :]
        for part in range(2):
            accd[part] += jnp.dot(t[:, part * 256 : part * 256 + 256], d, preferred_element_type=F32)
        return carry

    lax.fori_loop(0, 8, early, 0)

    def source(slot, kind):
        moved = jnp.where(kind == 1, 3, jnp.where(kind == 2, 1, jnp.where(kind == 3, 2, 0)))
        return (col + moved) % 4, (1 - z_hi) * 2 + jnp.where(slot == 2, core, 1 - core)

    def late(u, carry):
        @pl.when(u == 1)
        def _():
            from_partner((0,), (0, 1, 2, 3))

        @pl.when(u == 2)
        def _():
            onward(3)
            arrive(5)

        @pl.when(u == 5)
        def _():
            from_partner((1, 2, 3), (0, 1, 2, 3))

        @pl.when(u == 6)
        def _():
            onward(4)
            arrive(6)

        @pl.when(u == 8)
        def _():
            onward(5)
            arrive(7)

        @pl.when(u == 9)
        def _():
            from_partner((0,), (4, 5, 6, 7))

        part = u // 8
        v = u % 8
        slot = jnp.where(v < 2, 2 + v, 2 + (v - 2) // 3)
        kind = jnp.where(v < 2, 0, 1 + (v - 2) % 3)
        quarter, owner = source(slot, kind)
        base = quarter * 512 + part * 256
        t = tok[:, pl.ds(pl.multiple_of(owner * ROWS + base, 256), 256)]
        acc[...] += jnp.dot(
            t, wbuf[slot, pl.ds(pl.multiple_of(base, 256), 256), :], preferred_element_type=F32)
        accd[part] += jnp.dot(
            t, dbuf[slot, pl.ds(pl.multiple_of(quarter * 256, 256), 256), :], preferred_element_type=F32)
        return carry

    lax.fori_loop(0, 10, late, 0)

    def last(u, carry):
        @pl.when(u == 1)
        def _():
            from_partner((1, 2, 3), (4, 5))
            onward(6)

        @pl.when(u == 3)
        def _():
            onward(7)

        @pl.when(u == 4)
        def _():
            from_partner((1, 2, 3), (6, 7))

        part = u // 3
        ts, ws, ds = [], [], []
        for n in range(2):
            i = 2 * (u % 3) + n
            slot = 2 + i // 3
            quarter, owner = source(slot, 1 + i % 3)
            base = quarter * 512 + 256 + part * 128
            ts.append(tok[:, pl.ds(pl.multiple_of(owner * ROWS + base, 128), 128)])
            ws.append(wbuf[slot, pl.ds(pl.multiple_of(base, 128), 128), :])
            ds.append(dbuf[slot, pl.ds(pl.multiple_of(quarter * 256 + part * 128, 128), 128), :])
        t = jnp.concatenate(ts, axis=1)
        acc[...] += jnp.dot(t, jnp.concatenate(ws, axis=0), preferred_element_type=F32)
        accd[1] += jnp.dot(t, jnp.concatenate(ds, axis=0), preferred_element_type=F32)
        return carry

    lax.fori_loop(0, 6, last, 0)

    low = (accd[0] + pltpu.roll(accd[1], 64, 1)).astype(BF16)[:, :RANK]
    start0, start1 = pos[0, 0], pos[0, HALF]
    swap = start0 > start1
    lower = jnp.where(swap, start1, start0)
    pair = jnp.where(iota((HD, 2 * HD), 0) == iota((HD, 2 * HD), 1) % HD, 1.0, 0.0).astype(BF16)

    def joined(t):
        cols = slice(t * HD, (t + 1) * HD)
        full = acc[:, cols] + jnp.dot(low, up[:, cols], preferred_element_type=F32)
        high = full.astype(BF16)
        rest = (full - high.astype(F32)).astype(BF16)
        return lax.dot_general(pair, jnp.concatenate([high, rest], axis=1), NT, preferred_element_type=F32)

    def rope(u, k):
        c, n = cos_ref[16 * k : 16 * k + 16, :], sin_ref[16 * k : 16 * k + 16, :]
        return jnp.concatenate([u[:16] * c - u[16:] * n, u[16:] * c + u[:16] * n], axis=0)

    def halves(a, axis):
        lo = lax.slice_in_dim(a, 0, HALF, axis=axis)
        hi = lax.slice_in_dim(a, HALF, TOK, axis=axis)
        return jnp.where(swap, hi, lo), jnp.where(swap, lo, hi)

    ahead = joined(0)
    for j in range(2):
        for k in range(4):
            turned = ahead
            ahead = joined(4 * j + k + 1)
            for t in range(4):
                q = (rope(turned[32 * t : 32 * t + 32], k) * HD ** (-0.5)).astype(BF16).astype(F32) * LOG2E
                for s, part in enumerate(halves(q, 1)):
                    high = part.astype(BF16)
                    rest = (part - high.astype(F32)).astype(BF16)
                    for n in range(2):
                        tile = 2 * (4 * j + t) + n
                        q_out[s, tile, 32 * k : 32 * k + 32, :] = high[:, n * 128 : n * 128 + 128]
                        q_out[s, tile, HD + 32 * k : HD + 32 * k + 32, :] = rest[:, n * 128 : n * 128 + 128]
    both = (ahead, joined(9))
    key = jnp.concatenate(
        [rope(both[k // 2][64 * (k % 2) : 64 * (k % 2) + 32], k) for k in range(4)], axis=0)
    for s, part in enumerate(halves(key.T, 0)):
        kv_out[s, :HALF, :] = part.astype(BF16)
    value = jnp.concatenate(
        [both[k // 2][64 * (k % 2) + 32 : 64 * (k % 2) + 64] for k in range(4)], axis=0).astype(BF16)
    vt = jnp.dot(head_order(), value, preferred_element_type=F32)
    for s, part in enumerate(halves(vt, 1)):
        kv_out[s, HALF : HALF + 128, :] = part[:, :128].astype(BF16)
        kv_out[s, HALF + 128 : HALF + 256, :] = part[:, 128:].astype(BF16)
        kv_out[s, 2 * HALF :, :] = (jnp.zeros((META, HD), F32) + (lower // HALF).astype(F32)).astype(BF16)

    for kind in range(9):
        for c in range(4 if kind == 4 else 8):
            w_of(kind, c).wait_send()
    for kind in range(9):
        d_of(kind).wait_send()


def project(pos, tokens, codes, scales, down, up):
    view = codes.reshape(4, 8, 160, HD).transpose(0, 2, 1, 3).reshape(5120, HD)
    anywhere = pl.BlockSpec(memory_space=pl.ANY)
    vmem = pl.BlockSpec(memory_space=pltpu.VMEM)
    dma = pltpu.SemaphoreType.DMA
    return pl.pallas_call(
        project_kernel,
        out_shape=(
            jax.ShapeDtypeStruct((2, 2 * QH, 2 * HD, 128), BF16),
            jax.ShapeDtypeStruct((2, PIECE, HD), BF16),
        ),
        in_specs=[pl.BlockSpec(memory_space=pltpu.SMEM), anywhere, anywhere, vmem, anywhere, vmem],
        out_specs=(vmem, vmem),
        scratch_shapes=[
            pltpu.VMEM((4, ROWS, OUT), BF16),
            pltpu.VMEM((4, ROWS // 2, HD), BF16),
            pltpu.VMEM((TOK, WIDTH), BF16),
            pltpu.VMEM((TOK, OUT), F32),
            pltpu.VMEM((2, TOK, HD), F32),
            pltpu.VMEM((64, TOK), F32),
            pltpu.VMEM((64, TOK), F32),
            pltpu.VMEM((5120, HD), jnp.int32),
            pltpu.VMEM((2, 3, 64, HD), jnp.int32),
            pltpu.VMEM((HEADS, 32, HD), F32),
            pltpu.VMEM((RANK, OUT), BF16),
            dma((2,)), dma((4,)), dma((9, 8)), dma((9, 8)), dma((9,)), dma((9,)),
        ],
        compiler_params=pltpu.CompilerParams(
            collective_id=0, has_side_effects=True, vmem_limit_bytes=60 << 20),
        name="project",
    )(pos, tokens, view, scales, down, up)


ARRIVE = (
    ((0, 0, 0), None, None),
    ((0, 0, 1), "yp", "yp"),
    ((0, 3, 0), "xm", "xm"),
    ((0, 1, 0), "xp", "xp"),
    ((0, 0, 3), "ym", "ym"),
    ((0, 3, 1), "yp", "xm"),
    ((1, 0, 0), "z", "z"),
    ((0, 1, 1), "yp", "xp"),
    ((0, 2, 0), "xp", "xm"),
    ((0, 1, 3), "ym", "xp"),
    ((0, 3, 3), "xm", "ym"),
    ((1, 1, 0), "xp", "z"),
    ((1, 0, 1), "z", "yp"),
    ((1, 3, 0), "z", "xm"),
    ((0, 0, 2), "ym", "ym"),
    ((1, 1, 1), "yp", "z"),
    ((1, 0, 3), "ym", "ym"),
    ((0, 2, 1), "yp", "xm"),
    ((0, 2, 3), "xp", "xp"),
    ((1, 3, 1), "xm", "xm"),
    ((1, 2, 0), "z", "xp"),
    ((0, 3, 2), "xm", "ym"),
    ((1, 0, 2), "yp", "z"),
    ((0, 1, 2), "yp", "xp"),
    ((1, 3, 3), "ym", "z"),
    ((1, 1, 2), "yp", "yp"),
    ((1, 2, 3), "z", "ym"),
    ((1, 2, 1), "xm", "xm"),
    ((1, 1, 3), "z", "xp"),
    ((1, 3, 2), "z", "ym"),
    ((0, 2, 2), "xp", "yp"),
    ((1, 2, 2), "ym", "xp"),
)
ORDER = tuple(entry[0] for entry in ARRIVE)
SLOT = {s: i for i, s in enumerate(ORDER)}
BLOCKS = len(ORDER)
PAIRS = BLOCKS // 2


def routes():
    steps = {"xp": (0, -1, 0), "xm": (0, 1, 0), "yp": (0, 0, -1), "ym": (0, 0, 1), "z": (1, 0, 0)}
    table = {}
    for (dz, dx, dy), *origins in ARRIVE[1:]:
        for p, origin in enumerate(origins):
            sz, sx, sy = steps[origin]
            table[(dz, dx, dy), p] = (origin, ((dz + sz) % 2, (dx + sx) % 4, (dy + sy) % 4))
    return table


def forwards():
    opposite = {"xp": "xm", "xm": "xp", "yp": "ym", "ym": "yp", "z": "z"}
    table = {i: [] for i in range(BLOCKS)}
    for (s, p), (origin, source) in routes().items():
        table[SLOT[source]].append((SLOT[s], p, opposite[origin]))
    return {i: sorted(v) for i, v in table.items()}


def attend_kernel(pos, q_in, kv, out, kvbuf, q, k2, vt1, vt2, m_ref, acc, local, send, recv):
    z_hi, core, z_lo, x, y = place()
    peers = {
        "xp": device(z_hi, core, z_lo, x + 1, y), "xm": device(z_hi, core, z_lo, x + 3, y),
        "yp": device(z_hi, core, z_lo, x, y + 1), "ym": device(z_hi, core, z_lo, x, y + 3),
        "z": device(z_hi, core, 1 - z_lo, x, y),
    }
    table = forwards()
    own = pltpu.make_async_copy(kv, kvbuf.at[0], local.at[0])
    own_q = pltpu.make_async_copy(q_in, q, local.at[1])
    own.start()
    own_q.start()
    barrier = pltpu.get_barrier_semaphore()
    for peer in peers.values():
        pl.semaphore_signal(barrier, inc=1, device_id=peer, device_id_type=MESH)
    pl.semaphore_wait(barrier, len(peers))
    own.wait()

    def copy(source, slot, piece, peer):
        return pltpu.make_async_remote_copy(
            src_ref=kvbuf.at[source, piece], dst_ref=kvbuf.at[slot, piece],
            send_sem=send.at[slot, piece], recv_sem=recv.at[slot, piece],
            device_id=peer, device_id_type=MESH,
        )

    def forward(source):
        for slot, piece, to in table[source]:
            copy(source, slot, piece, peers[to]).start()

    def take(slot):
        for piece in range(2):
            copy(0, slot, piece, peers["z"]).wait_recv()

    forward(0)

    start0, start1 = pos[0, 0], pos[0, HALF]
    swap = start0 > start1
    mine = (jnp.where(swap, start1, start0) // HALF).astype(F32)
    one = jnp.ones((META, HALF), BF16)
    for n in range(2):
        vt1[n, HD:, :HALF] = one
        vt2[n, HD:, :] = one

    def query(s, h):
        return jnp.concatenate([q[s, 2 * h], q[s, 2 * h + 1]], axis=1)

    def keys(slot, piece):
        return kvbuf[slot, piece, :HALF, :]

    def values(slot, piece):
        return jnp.concatenate(
            [kvbuf[slot, piece, HALF : HALF + 128, :], kvbuf[slot, piece, HALF + 128 : HALF + 256, :]], axis=1)

    def scores(k, qt):
        return jnp.dot(jnp.concatenate([k, k], axis=1), qt, preferred_element_type=F32)

    def top(s):
        return jnp.max(s, axis=0, keepdims=True)

    own_q.wait()
    def pipeline(units, product, soften, gather):
        ahead, ready = product(*units[0]), None
        for n, unit in enumerate(units):
            now = ahead
            if n + 1 < len(units):
                ahead = product(*units[n + 1])
            if ready is not None:
                gather(*units[n - 1], *ready)
            ready = soften(*unit, *now)
        gather(*units[-1], *ready)

    vt1[0, :HD, :HALF] = values(0, 0)
    vt2[0, :HD, :] = values(0, 1)
    k2[0] = keys(0, 1)
    seen = iota((HALF, HALF), 0) <= iota((HALF, HALF), 1)

    def own_product(h):
        q0, q1 = query(0, h), query(1, h)
        return scores(keys(0, 0), q0), scores(keys(0, 0), q1), scores(k2[0], q1)

    def own_soften(h, s00, s10, s11):
        s00, s11 = jnp.where(seen, s00, -jnp.inf), jnp.where(seen, s11, -jnp.inf)
        m0, m1 = top(s00), jnp.maximum(top(s10), top(s11))
        m_ref[0, h] = jnp.broadcast_to(m0, (8, HALF))
        m_ref[1, h] = jnp.broadcast_to(m1, (8, HALF))
        return [jnp.exp2(x - m).astype(BF16) for x, m in ((s00, m0), (s10, m1), (s11, m1))]

    def own_gather(h, e00, e10, e11):
        def weigh(vt, e):
            return jnp.dot(vt, e, preferred_element_type=F32)

        acc[0, h] = weigh(vt1[0, :, :HALF], e00)
        acc[1, h] = weigh(vt1[0, :, :HALF], e10) + weigh(vt2[0], e11)

    pipeline([(h,) for h in range(QH)], own_product, own_soften, own_gather)

    def blocks(slots):
        low, lo_bias, hi_bias = [], [], []
        zero = jnp.zeros((HD, HALF), BF16)
        for n, i in enumerate(slots):
            c = jnp.max(kvbuf[i, 0, 2 * HALF :, :].astype(F32)) < mine
            low.append(c)
            lo_bias.append(jnp.where(c, 0.0, NEG))
            hi_bias.append(jnp.where(c, NEG, 0.0))
            low_v = values(i, 0)
            k2[n] = jnp.where(c, keys(i, 0), keys(i, 1))
            vt1[n, :HD, :HALF] = low_v
            vt1[n, :HD, HALF:] = jnp.where(c, zero, values(i, 1))
            vt1[n, HD:, HALF:] = jnp.where(c, zero[:META], one)
            vt2[n, :HD, :] = jnp.where(c, low_v, zero)
            vt2[n, HD:, :] = jnp.where(c, one, zero[:META])

        def product(n, h):
            q1 = query(1, h)
            q2 = jnp.where(low[n], query(0, h), q1)
            return scores(keys(slots[n], 0), q1), scores(k2[n], q2)

        def soften(n, h, s1, s2):
            t1, t2 = top(s1), top(s2)
            m_lo, m_hi = m_ref[0, h, :1, :], m_ref[1, h, :1, :]
            n_lo = jnp.maximum(m_lo, t2 + lo_bias[n])
            n_hi = jnp.maximum(m_hi, jnp.maximum(t1, t2 + hi_bias[n]))
            e1 = jnp.exp2(s1 - n_hi).astype(BF16)
            e2 = jnp.exp2(s2 - jnp.where(low[n], n_lo, n_hi)).astype(BF16)
            m_ref[0, h] = jnp.broadcast_to(n_lo, (8, HALF))
            m_ref[1, h] = jnp.broadcast_to(n_hi, (8, HALF))
            return e1, e2, jnp.exp2(m_lo - n_lo), jnp.exp2(m_hi - n_hi)

        def gather(n, h, e1, e2, f_lo, f_hi):
            o_hi = jnp.dot(vt1[n], jnp.concatenate([e1, e2], axis=0), preferred_element_type=F32)
            o_lo = jnp.dot(vt2[n], e2, preferred_element_type=F32)
            acc[0, h] = acc[0, h] * f_lo + o_lo
            acc[1, h] = acc[1, h] * f_hi + o_hi

        pipeline([(n, h) for n in range(len(slots)) for h in range(QH)], product, soften, gather)

    def step(p, carry):
        def come(k):
            @pl.when(p + 1 == k)
            def _():
                for slot in (2 * k - 1, 2 * k):
                    if slot < BLOCKS:
                        take(slot)
                        forward(slot)

        for group in range(0, PAIRS + 1, 4):
            @pl.when((p + 1 >= group) & (p + 1 < group + 4))
            def _():
                for k in range(max(group, 1), min(group + 4, PAIRS + 1)):
                    come(k)

        @pl.when(p > 0)
        def _():
            blocks((2 * p - 1, 2 * p))

        return carry

    lax.fori_loop(0, PAIRS, step, 0)
    blocks((BLOCKS - 1,))

    for h in range(QH):
        cols = slice(h * HD, (h + 1) * HD)
        parts = []
        for s in range(2):
            total = acc[s, h, HD : HD + 1, :]
            parts.append((acc[s, h, :HD, :] / total).T)
        out[:HALF, cols] = jnp.where(swap, parts[1], parts[0]).astype(BF16)
        out[HALF:, cols] = jnp.where(swap, parts[0], parts[1]).astype(BF16)

    def drain(slot, carry):
        for piece in range(2):
            copy(0, slot, piece, peers["z"]).wait_send()
        return carry

    lax.fori_loop(1, BLOCKS, drain, 0)


def attend(pos, q, kv):
    anywhere = pl.BlockSpec(memory_space=pl.ANY)
    vmem = pl.BlockSpec(memory_space=pltpu.VMEM)
    dma = pltpu.SemaphoreType.DMA
    return pl.pallas_call(
        attend_kernel,
        out_shape=jax.ShapeDtypeStruct((TOK, QH * HD), BF16),
        in_specs=[pl.BlockSpec(memory_space=pltpu.SMEM), anywhere, anywhere],
        out_specs=vmem,
        scratch_shapes=[
            pltpu.VMEM((BLOCKS, 2, PIECE, HD), BF16),
            pltpu.VMEM((2, 2 * QH, 2 * HD, 128), BF16),
            pltpu.VMEM((2, HALF, HD), BF16),
            pltpu.VMEM((2, HD + META, 2 * HALF), BF16),
            pltpu.VMEM((2, HD + META, HALF), BF16),
            pltpu.VMEM((2, QH, 8, HALF), F32),
            pltpu.VMEM((2, QH, HD + META, HALF), F32),
            dma((2,)), dma((BLOCKS, 2)), dma((BLOCKS, 2)),
        ],
        compiler_params=pltpu.CompilerParams(
            collective_id=1, has_side_effects=True, vmem_limit_bytes=60 << 20),
        name="attend",
    )(pos, q, kv)


def on_device(tokens, codes, scales, down_adapter_matrix, up_adapter_matrix, positions):
    down = down_adapter_matrix.reshape(4, 2, HALF, RANK).transpose(0, 2, 1, 3).reshape(ROWS // 2, HD)
    q, kv = project(positions, tokens[0], codes, scales, down, up_adapter_matrix)
    return attend(positions, q, kv)[None]


def solution(mesh):
    return jax.shard_map(
        on_device,
        mesh=mesh,
        in_specs=(
            P("fsdp", "ctx", None), P("fsdp", None), P("fsdp", None), P("fsdp", None), P(), P("fsdp", "ctx"),
        ),
        out_specs=P("fsdp", "ctx", None),
        check_vma=False,
    )
```
